512 devices in a mesh: de: 32 (over x, y_lo, core), et: 16 (over y_hi, z).
Axes of the slice: x: 4, y: 8 (y_hi: 2, y_lo: 4; y = y_hi * 4 + y_lo), z: 8, core: 2. Of those that a mesh axis runs over, the one named last changes fastest.
Arguments:
- tokens: bfloat16 [256, 6144], P('de', 'et'), may hold values from -6 to 6
- expert_ids: int32 [256, 2], P('de'), may hold values from 0 to 3, all different within a row; in each aligned block of 8 rows (0 to 7, 8 to 15, ...) at most 5 rows name the same one
- gate_probs: float32 [256, 2], P('de'), may hold values from 0.1 to 1
- w_gate: bfloat16 [6144, 65536], P(None, ('de', 'et')), may hold values from -0.078125 to 0.078125
- w_up: bfloat16 [6144, 65536], P(None, ('de', 'et')), may hold values from -0.078125 to 0.078125
- w_down: bfloat16 [65536, 6144], P(('de', 'et')), may hold values from -0.046875 to 0.046875
- out_grad: bfloat16 [256, 6144], P('de', 'et'), may hold values from -6 to 6
Outputs:
- mixed: bfloat16 [256, 6144], P('de', 'et')
- token_grad: bfloat16 [256, 6144], P('de', 'et')
- prob_grad: float32 [256, 2], P('de')
The draws below stay inside these ranges and needn't reach their ends.
Inputs may be any that keep to these rules, and one draw needn't show every extreme that they name: `expert_ids`: the 2 entries of a token are different. Among the 8 tokens of one index of de, no expert is named by more than 5 tokens, a bound that some expert reaches in some of these blocks.
All inputs are finite; a program needn't handle non-finite values.
Results may differ from the reference program's by a relative error of at most 0.02.
Values may be sent and summed in bfloat16 or wider, within the bound.
A program may use at most 64 MiB of HBM per device.

```python
import math
import jax
import jax.numpy as jnp
import numpy as np
from jax import lax

D = 6144
FF = 16384
EXPERTS = 4
TOP = 2
TOK_DE = 8
CAP = 5
TOKENS = 256
N_DE = 32
N_ET = 16


def steps_of(key, shape, split, low, high):
    loudness = 1.0
    for position, parts in split:
        heights = jax.random.uniform(jax.random.fold_in(jax.random.fold_in(key, 6), position), (parts,), jnp.float32, low / len(split), high / len(split))
        loudness = loudness * jnp.repeat(jnp.exp(heights), shape[position] // parts).reshape((-1,) + (1,) * (len(shape) - 1 - position))
    return loudness


def deal_out(rng, own, number, rows, number_of, top, reach, lean):
    order = jax.random.permutation(rng, number_of)
    crowded, usual = shares(number_of, rows * top, reach, lean, True), shares(number_of, rows * top, reach, lean, False)
    places = jnp.arange(number_of)

    def named(sizes, turn):
        used = int((sizes > 0).sum())
        fixed = max(1, used // 4)
        moved = fixed + (places - fixed + turn * (used - fixed)) % max(1, number_of - fixed)
        return jnp.zeros((number_of,), jnp.int32).at[order[jnp.where(places < fixed, places, moved)]].set(jnp.asarray(sizes, jnp.int32))

    sizes = jnp.where(number % 4 == 0, named(crowded, number // 4), named(usual, number - number // 4 - 1))
    mixed = jax.random.permutation(jax.random.fold_in(own, 3), number_of)
    source_of, sink = mixed[0:number_of // 2 * 2:2], mixed[1:number_of // 2 * 2:2]
    slack = jnp.minimum(sizes[source_of] - 1, reach - sizes[sink]) // 2
    slack = jnp.where((source_of == order[0]) | (sink == order[0]) | (sizes[sink] == 0), 0, jnp.maximum(slack, 0))
    moved = jax.random.randint(jax.random.fold_in(own, 4), (number_of // 2,), 0, 1 << 20) % (slack + 1)
    sizes = sizes.at[source_of].add(-moved).at[sink].add(moved)
    items = jnp.searchsorted(jnp.cumsum(sizes), jnp.arange(rows * top), side="right").astype(jnp.int32)
    table = items.reshape(top, rows).T
    table = table[jax.random.permutation(jax.random.fold_in(own, 1), rows)]
    turn = jax.random.randint(jax.random.fold_in(own, 2), (rows, 1), 0, top)
    return jnp.take_along_axis(table, (jnp.arange(top)[None, :] + turn) % top, axis=1)


def shares(amount, total, reach, lean, full):
    weights = [(1 << 20) // math.isqrt(rank ** lean) + 1 for rank in range(1, amount + 1)]
    largest = reach if full else min(reach, max(-(-total // amount), total * weights[0] // sum(weights)))
    least = 1 if total - largest >= amount - 1 else 0
    counts, rest = [largest] + [least] * (amount - 1), total - largest - least * (amount - 1)
    while rest > 0:
        movable = [i for i in range(1, amount) if counts[i] < largest] or [i for i in range(1, amount) if counts[i] < reach]
        whole, budget = sum([weights[i] for i in movable]), rest
        for i in movable:
            extra = min(reach - counts[i], max(1, budget * weights[i] // whole), rest)
            counts[i] = counts[i] + extra
            rest = rest - extra
    return np.array(counts)


def gaussian(rng, dims, width, reach, split=(), kind=jnp.bfloat16):
    loudness = steps_of(rng, dims, split, -0.22, 0.18) if split else 1.0
    values = jax.random.normal(rng, dims, jnp.float32) * width * loudness
    return jnp.minimum(jnp.maximum(values, -reach), reach).astype(kind)


def setup_inputs(seed: int = 0) -> dict:
    streams_of = jax.random.split(jax.random.key(seed), 8)
    tokens = gaussian(streams_of[0], (TOKENS, D), 1.0, 6.0, ((0, 32), (1, 16)))
    expert_ids_keys = jax.random.split(jax.random.fold_in(streams_of[1], 1), TOKENS // TOK_DE)
    expert_ids_turns = jax.random.permutation(jax.random.fold_in(streams_of[1], 3), TOKENS // TOK_DE)
    expert_ids = jax.vmap(lambda own, number: deal_out(jax.random.fold_in(streams_of[1], 2), own, number, TOK_DE, EXPERTS, TOP, CAP, 2))(expert_ids_keys, expert_ids_turns).reshape((TOKENS, TOP))
    gate_probs = jnp.clip(0.1 + 0.9 * jax.random.uniform(streams_of[2], (TOKENS, TOP), jnp.float32) ** steps_of(streams_of[2], (TOKENS, TOP), ((0, 32),), -0.2, 0.2), 0.1, 1.0)
    w_gate = gaussian(streams_of[3], (D, EXPERTS * FF), D ** -0.5, 0.078125, ((1, 512),))
    w_up = gaussian(streams_of[4], (D, EXPERTS * FF), D ** -0.5, 0.078125, ((1, 512),))
    w_down = gaussian(streams_of[5], (EXPERTS * FF, D), FF ** -0.5, 0.046875, ((0, 512),))
    out_grad = gaussian(streams_of[6], (TOKENS, D), 1.0, 6.0, ((0, 32), (1, 16)))
    return dict(tokens=tokens, expert_ids=expert_ids, gate_probs=gate_probs, w_gate=w_gate, w_up=w_up, w_down=w_down, out_grad=out_grad)


def blocked_terms(hidden, d_gate, d_up, wg, wu, wd, blocks, hid):
    rows = hidden.shape[0]
    hid_blocks = hidden.reshape(rows, blocks, hid).transpose(1, 0, 2)
    dg_blocks = d_gate.reshape(rows, blocks, hid).transpose(1, 0, 2)
    du_blocks = d_up.reshape(rows, blocks, hid).transpose(1, 0, 2)
    wd_blocks = wd.reshape(blocks, hid, D)
    wg_blocks = wg.reshape(D, blocks, hid).transpose(1, 0, 2)
    wu_blocks = wu.reshape(D, blocks, hid).transpose(1, 0, 2)

    def step(carry, item):
        hpart, wdk, gpart, upart, wgk, wuk = item
        yk = jnp.dot(hpart, wdk, preferred_element_type=jnp.float32)
        yk = lax.optimization_barrier(yk.astype(jnp.bfloat16)).astype(jnp.float32)
        xk = lax.dot_general(gpart, wgk, (((1,), (1,)), ((), ())), preferred_element_type=jnp.float32)
        xk = xk + lax.dot_general(upart, wuk, (((1,), (1,)), ((), ())), preferred_element_type=jnp.float32)
        xk = lax.optimization_barrier(xk.astype(jnp.bfloat16)).astype(jnp.float32)
        return (carry[0] + yk, carry[1] + xk), None

    start = (jnp.zeros((rows, D), jnp.float32), jnp.zeros((rows, D), jnp.float32))
    (ye, dxe), unused = lax.scan(step, start, (hid_blocks, wd_blocks, dg_blocks, du_blocks, wg_blocks, wu_blocks))
    return ye, dxe


def reference(tokens, expert_ids, gate_probs, w_gate, w_up, w_down, out_grad):
    rows = N_DE * CAP
    blocks = N_ET * (N_DE // EXPERTS)
    hid = FF // blocks
    picks = (expert_ids[:, :, None] == jnp.arange(EXPERTS, dtype=jnp.int32)[None, None, :]).astype(jnp.int32)
    named = jnp.sum(picks, axis=1)
    weight = jnp.sum(picks.astype(jnp.float32) * gate_probs[:, :, None], axis=1)
    rank = jnp.cumsum(named.reshape(N_DE, TOK_DE, EXPERTS), axis=1).reshape(TOKENS, EXPERTS) - 1
    source = jnp.arange(TOKENS, dtype=jnp.int32) // TOK_DE
    slot = jnp.where(named > 0, source[:, None] * CAP + rank, rows).astype(jnp.int32)
    grad_f = out_grad.astype(jnp.float32)
    mixed = jnp.zeros((TOKENS, D), jnp.float32)
    token_grad = jnp.zeros((TOKENS, D), jnp.float32)
    scores = []
    for expert in range(EXPERTS):
        index = slot[:, expert]
        xe = jnp.zeros((rows + 1, D), jnp.bfloat16).at[index].set(tokens)[:rows]
        scaled = (weight[:, expert:expert + 1] * grad_f).astype(jnp.bfloat16)
        ge = jnp.zeros((rows + 1, D), jnp.bfloat16).at[index].set(scaled)[:rows]
        wg = w_gate[:, expert * FF:(expert + 1) * FF]
        wu = w_up[:, expert * FF:(expert + 1) * FF]
        wd = w_down[expert * FF:(expert + 1) * FF]
        gate = jnp.dot(xe, wg, preferred_element_type=jnp.float32)
        up = jnp.dot(xe, wu, preferred_element_type=jnp.float32)
        sig = jax.nn.sigmoid(gate)
        hidden = (gate * sig * up).astype(jnp.bfloat16)
        d_hidden = lax.dot_general(ge, wd, (((1,), (1,)), ((), ())), preferred_element_type=jnp.float32)
        d_gate = (d_hidden * up * sig * (1.0 + gate * (1.0 - sig))).astype(jnp.bfloat16)
        d_up = (d_hidden * gate * sig).astype(jnp.bfloat16)
        ye, dxe = blocked_terms(hidden, d_gate, d_up, wg, wu, wd, blocks, hid)
        take = jnp.minimum(index, rows - 1).astype(jnp.int32)
        live = named[:, expert:expert + 1].astype(jnp.float32)
        y_rows = ye[take] * live
        mixed = mixed + weight[:, expert:expert + 1] * y_rows
        token_grad = token_grad + dxe[take] * live
        scores.append(jnp.sum(grad_f * y_rows, axis=1))
    score_table = jnp.stack(scores, axis=1)
    prob_grad = jnp.sum(picks.astype(jnp.float32) * score_table[:, None, :], axis=2)
    return mixed.astype(jnp.bfloat16), token_grad.astype(jnp.bfloat16), prob_grad
```

```python
import functools

import jax
import jax.numpy as jnp
from jax import lax
from jax.experimental import pallas as pl
from jax.experimental.pallas import tpu as pltpu
from jax.sharding import PartitionSpec as P

EXPERTS = 4
CAP = 5
SLOT = 8
Y_HI = 2
MESH = pl.DeviceIdType.MESH
F32 = jnp.float32
BF16 = jnp.bfloat16
HIGHEST = lax.Precision.HIGHEST


def dot(a, b, contract, precision=None):
    return lax.dot_general(
        a, b, ((contract[0], contract[1]), ((), ())), preferred_element_type=F32, precision=precision
    )


def fifth(p):
    return (p * 13) >> 6


def kernel(
    sizes,
    ids_ref,
    probs_ref,
    tok_ref,
    grad_ref,
    wg_hbm,
    wu_hbm,
    wd_hbm,
    mixed_ref,
    tgrad_ref,
    pgrad_ref,
    wgu,
    wdv,
    s1,
    r1,
    gb,
    acc_gu,
    acc_d,
    hid,
    dgu,
    tb,
    sr,
    rr,
    p2,
    s2,
    r2,
    pg,
    w_sem,
    s1_s,
    s1_r,
    p1_s,
    p1_r,
    ag_s,
    ag_r,
    sh_s,
    sh_r,
    st_s,
    st_r,
    rs_s,
    rs_r,
    p2_s,
    p2_r,
    s2_s,
    s2_r,
    pg_s,
    pg_r,
):
    nx, yl, n = sizes
    n2 = n // 2
    group = 2 * nx
    rows = group * CAP
    width = tok_ref.shape[1]
    hidden_units = wdv.shape[0]
    de, et = lax.axis_index("de"), lax.axis_index("et")
    c = lax.rem(de, 2)
    y_lo = lax.rem(lax.div(de, 2), yl)
    x = lax.div(de, 2 * yl)
    y_hi, z = lax.div(et, n), lax.rem(et, n)
    y = y_hi * yl + y_lo
    me = x * 2 + c
    b0 = jnp.where(c == 0, y, z)
    a0 = jnp.where(c == 0, z, y)

    def wrap(v, m):
        return lax.rem(v + m, m)

    def device(x_, y_, z_, c_):
        return ((x_ * yl + lax.rem(y_, yl)) * 2 + c_, lax.div(y_, yl) * n + z_)

    def at_ba(b_, a_):
        return device(x, jnp.where(c == 0, b_, a_), jnp.where(c == 0, a_, b_), c)

    def at_group(idx):
        return device(lax.div(idx, 2), y, z, lax.rem(idx, 2))

    sibling = device(x, y, z, 1 - c)
    onward = (at_ba(wrap(b0 + 1, n), a0), at_ba(wrap(b0 - 1, n), a0))
    sends = []

    def send(src, dst, s_sem, r_sem, to):
        copy = pltpu.make_async_remote_copy(
            src_ref=src, dst_ref=dst, send_sem=s_sem, recv_sem=r_sem, device_id=to, device_id_type=MESH
        )
        copy.start()
        sends.append(copy)

    def arrived(dst, sem):
        pltpu.make_async_copy(dst, dst, sem).wait()

    loads = (
        pltpu.make_async_copy(wg_hbm, wgu.at[:, pl.ds(0, hidden_units)], w_sem.at[0]),
        pltpu.make_async_copy(wu_hbm, wgu.at[:, pl.ds(hidden_units, hidden_units)], w_sem.at[1]),
        pltpu.make_async_copy(wd_hbm, wdv, w_sem.at[2]),
    )
    for load in loads:
        load.start()

    barrier = pltpu.get_barrier_semaphore()
    peers = [at_group(wrap(me + i, group)) for i in range(1, group)]
    for i in range(1, n):
        peers.append(device(x, y, wrap(z + i, n), c))
        peers.append(device(x, wrap(y + i, n), z, c))
        peers.append(device(x, wrap(y + yl, n), wrap(z + i, n), c))
    for peer in peers:
        pl.semaphore_signal(barrier, inc=1, device_id=peer, device_id_type=MESH)

    ids, probs = ids_ref[...], probs_ref[...]
    tokens = ids.shape[0]
    lane = lax.broadcasted_iota(jnp.int32, (tokens, 128), 1)
    row = lax.broadcasted_iota(jnp.int32, (tokens, 128), 0)
    named = jnp.where((ids[:, 0:1] == lane) | (ids[:, 1:2] == lane), 1.0, 0.0)
    rank = jnp.zeros((tokens, 128), F32)
    for t in range(tokens - 1):
        rank = rank + jnp.where(row > t, named[t : t + 1, :], 0.0)
    sel = []
    for j in range(2):
        e = ids[:, j : j + 1]
        rank_j = jnp.sum(jnp.where(lane == e, rank, 0.0), axis=1, keepdims=True)
        slot = e.astype(F32) * SLOT + rank_j
        sel.append(jnp.where(lane.astype(F32) == slot, 1.0, 0.0)[:, : nx * SLOT])
    tok_f, grad_f = tok_ref[...].astype(F32), grad_ref[...].astype(F32)
    first = ((0,), (0,))
    xs = dot(sel[0] + sel[1], tok_f, first, HIGHEST)
    gs = jnp.zeros_like(xs)
    for j in range(2):
        scaled = (probs[:, j : j + 1] * grad_f).astype(BF16).astype(F32)
        gs = gs + dot(sel[j], scaled, first, HIGHEST)
    for e in range(nx):
        block = slice(e * SLOT, (e + 1) * SLOT)
        s1[e] = jnp.concatenate([xs[block], gs[block]], axis=0).astype(BF16)

    pl.semaphore_wait(barrier, len(peers))

    for i in range(1, group):
        to = wrap(me + i, group)
        send(s1.at[lax.div(to, 2)], r1.at[me], s1_s.at[i], s1_r.at[i], at_group(to))
    r1[me] = s1[x]
    for i in range(1, group):
        arrived(r1.at[wrap(me - i, group)], s1_r.at[i])
    p = lax.broadcasted_iota(jnp.int32, (rows, group * 16), 0)
    col = lax.broadcasted_iota(jnp.int32, (rows, group * 16), 1)
    pick = jnp.where(col == p + 11 * fifth(p) + 8 * c, 1.0, 0.0).astype(BF16)
    staged = r1[...].reshape(group * 16, width)
    gb[c, b0, a0] = dot(pick, staged, ((1,), (0,))).astype(BF16)

    for i in range(1, n):
        send(gb.at[c, b0, a0], gb.at[c, b0, a0], p1_s.at[i], p1_r.at[a0], at_ba(b0, wrap(a0 + i, n)))

    def unit(b_, h):
        return gb.at[c, b_, pl.ds(h * n2, n2)]

    def share(b_, h):
        send(unit(b_, h), unit(b_, h), sh_s.at[b_, h], sh_r.at[b_, h], sibling)

    for h in range(2):
        for a_ in range(h * n2, (h + 1) * n2):

            @pl.when(a0 != a_)
            def _():
                arrived(gb.at[c, b0, a_], p1_r.at[a_])

        for d in range(2):
            send(unit(b0, h), unit(b0, h), ag_s.at[d, 0, h], ag_r.at[b0, h], onward[d])
        share(b0, h)
    for s in range(1, n2 + 1):
        for h in range(2):
            for d in range(2):
                if s == n2 and h != d:
                    continue
                b_ = wrap(b0 - s, n) if d == 0 else wrap(b0 + s, n)
                arrived(unit(b_, h), ag_r.at[b_, h])
                if s < n2 - 1 or (s == n2 - 1 and h == d):
                    send(unit(b_, h), unit(b_, h), ag_s.at[d, s, h], ag_r.at[b_, h], onward[d])
                share(b_, h)
    for b_ in range(n):
        for h in range(2):
            arrived(gb.at[1 - c, b_, pl.ds(h * n2, n2)], sh_r.at[b_, h])
    for load in loads:
        load.wait()

    acc_gu[...] = jnp.zeros_like(acc_gu)
    acc_d[...] = jnp.zeros_like(acc_d)

    @pl.loop(0, Y_HI * n)
    def _(q):
        hi, z_ = lax.div(q, n), lax.rem(q, n)
        span = pl.ds(pl.multiple_of(q * width, width), width)
        xq = jnp.concatenate([gb[0, hi * yl + k, z_] for k in range(yl)], axis=0)
        gq = jnp.concatenate([gb[1, z_, hi * yl + k] for k in range(yl)], axis=0)
        acc_gu[...] += dot(xq, wgu[span, :], ((1,), (0,)))
        acc_d[...] += dot(gq, wdv[:, span], ((1,), (1,)))

    gate, up, d_hidden = acc_gu[:, :hidden_units], acc_gu[:, hidden_units:], acc_d[...]
    sig = jax.nn.sigmoid(gate)
    hid[...] = (gate * sig * up).astype(BF16)
    dgu[:, :hidden_units] = (d_hidden * up * sig * (1.0 + gate * (1.0 - sig))).astype(BF16)
    dgu[:, hidden_units:] = (d_hidden * gate * sig).astype(BF16)

    def crossing(q, kind):
        hi, z_ = lax.div(q, n), lax.rem(q, n)
        part = pl.ds(hi * yl, yl)

        def copy(src, dst):
            return pltpu.make_async_remote_copy(
                src_ref=src,
                dst_ref=dst,
                send_sem=st_s.at[q],
                recv_sem=st_r.at[q],
                device_id=sibling,
                device_id_type=MESH,
            )

        if kind == 1:
            return copy(tb.at[1, z_, part], sr.at[z_, part])
        return copy(tb.at[0, part, z_], sr.at[part, z_])

    @pl.loop(0, Y_HI * n)
    def _(q):
        hi, z_ = lax.div(q, n), lax.rem(q, n)
        span = pl.ds(pl.multiple_of(q * width, width), width)
        yq = dot(hid[...], wdv[:, span], ((1,), (0,))).astype(BF16)
        xq = dot(dgu[...], wgu[span, :], ((1,), (1,))).astype(BF16)
        for k in range(yl):
            block = slice(k * rows, (k + 1) * rows)
            tb[0, hi * yl + k, z_] = yq[block]
            tb[1, z_, hi * yl + k] = xq[block]

        @pl.when(c == 0)
        def _():
            crossing(q, 1).start()

        @pl.when(c == 1)
        def _():
            crossing(q, 0).start()

    @pl.loop(0, Y_HI * n)
    def _(q):
        @pl.when(c == 0)
        def _():
            crossing(q, 1).wait_send()
            crossing(q, 0).wait_recv()

        @pl.when(c == 1)
        def _():
            crossing(q, 0).wait_send()
            crossing(q, 1).wait_recv()

    def half(h):
        return pl.ds(h * n2, n2)

    def own(t, h):
        return tb[c, t, half(h)].astype(F32) + sr[t, half(h)].astype(F32)

    for k in range(n2, 0, -1):
        for h in range(2):
            for d in range(2):
                if k == n2 and h != d:
                    continue
                t = wrap(b0 + k, n) if d == 0 else wrap(b0 - k, n)
                value = own(t, h)
                if k < n2 - 1 or (k == n2 - 1 and h == d):
                    arrived(rr.at[d, k, h], rs_r.at[d, k, h])
                    value = value + rr[d, k, h].astype(F32)
                tb[c, t, half(h)] = value.astype(BF16)
                send(
                    tb.at[c, t, half(h)],
                    rr.at[d, k - 1, h],
                    rs_s.at[d, k - 1, h],
                    rs_r.at[d, k - 1, h],
                    onward[d],
                )
    for h in range(2):
        value = own(b0, h)
        for d in range(2):
            arrived(rr.at[d, 0, h], rs_r.at[d, 0, h])
            value = value + rr[d, 0, h].astype(F32)
        tb[c, b0, half(h)] = value.astype(BF16)

    for i in range(1, n):
        to = wrap(a0 + i, n)
        send(tb.at[c, b0, to], p2.at[a0], p2_s.at[i], p2_r.at[i], at_ba(b0, to))
    total = tb[c, b0, a0].astype(F32)
    for i in range(1, n):
        a_ = wrap(a0 - i, n)
        arrived(p2.at[a_], p2_r.at[i])
        total = total + p2[a_].astype(F32)

    r = lax.broadcasted_iota(jnp.int32, (group * SLOT, rows), 0)
    p = lax.broadcasted_iota(jnp.int32, (group * SLOT, rows), 1)
    spread = jnp.where(r == p + 3 * fifth(p), 1.0, 0.0).astype(BF16)
    s2[...] = dot(spread, total.astype(BF16), ((1,), (0,))).reshape(group, SLOT, width).astype(BF16)
    for i in range(1, group):
        to = wrap(me + i, group)
        send(s2.at[to], r2.at[c, x], s2_s.at[i], s2_r.at[i], at_group(to))
    r2[c, x] = s2[me]
    for i in range(1, group):
        idx = wrap(me - i, group)
        arrived(r2.at[lax.rem(idx, 2), lax.div(idx, 2)], s2_r.at[i])

    last = ((1,), (0,))
    y_rows = r2[0].astype(F32).reshape(nx * SLOT, width)
    x_rows = r2[1].astype(F32).reshape(nx * SLOT, width)
    y_of = [dot(sel[j], y_rows, last, HIGHEST) for j in range(2)]
    part = jnp.zeros((tokens, 128), F32)
    for j in range(2):
        part = jnp.where(lane == j, jnp.sum(grad_f * y_of[j], axis=1, keepdims=True), part)
    pg[et] = part
    n_et = Y_HI * n
    for i in range(1, n_et):
        send(pg.at[et], pg.at[et], pg_s.at[i], pg_r.at[i], (de, wrap(et + i, n_et)))
    mixed_ref[...] = (probs[:, 0:1] * y_of[0] + probs[:, 1:2] * y_of[1]).astype(BF16)
    tgrad_ref[...] = dot(sel[0] + sel[1], x_rows, last, HIGHEST).astype(BF16)
    for i in range(1, n_et):
        arrived(pg.at[wrap(et - i, n_et)], pg_r.at[i])
    total = pg[0]
    for i in range(1, n_et):
        total = total + pg[i]
    pgrad_ref[...] = total[:, 0:2]
    for copy in sends:
        copy.wait_send()


def body(tokens, expert_ids, gate_probs, w_gate, w_up, w_down, out_grad):
    n_de, n_et = lax.axis_size("de"), lax.axis_size("et")
    nx = EXPERTS
    yl = n_de // (2 * nx)
    n = n_et // Y_HI
    n2 = n // 2
    group = 2 * nx
    rows = group * CAP
    count, width = tokens.shape
    depth, units = w_gate.shape
    slots = yl * rows
    vmem = pl.BlockSpec(memory_space=pltpu.VMEM)
    hbm = pl.BlockSpec(memory_space=pl.ANY)
    dma = pltpu.SemaphoreType.DMA
    return pl.pallas_call(
        functools.partial(kernel, (nx, yl, n)),
        out_shape=(
            jax.ShapeDtypeStruct((count, width), BF16),
            jax.ShapeDtypeStruct((count, width), BF16),
            jax.ShapeDtypeStruct(gate_probs.shape, F32),
        ),
        in_specs=[vmem] * 4 + [hbm] * 3,
        out_specs=(vmem, vmem, vmem),
        scratch_shapes=[
            pltpu.VMEM((depth, 2 * units), BF16),
            pltpu.VMEM((units, depth), BF16),
            pltpu.VMEM((nx, 16, width), BF16),
            pltpu.VMEM((group, 16, width), BF16),
            pltpu.VMEM((2, n, n, rows, width), BF16),
            pltpu.VMEM((slots, 2 * units), F32),
            pltpu.VMEM((slots, units), F32),
            pltpu.VMEM((slots, units), BF16),
            pltpu.VMEM((slots, 2 * units), BF16),
            pltpu.VMEM((2, n, n, rows, width), BF16),
            pltpu.VMEM((n, n, rows, width), BF16),
            pltpu.VMEM((2, n2, 2, n2, rows, width), BF16),
            pltpu.VMEM((n, rows, width), BF16),
            pltpu.VMEM((group, SLOT, width), BF16),
            pltpu.VMEM((2, nx, SLOT, width), BF16),
            pltpu.VMEM((n_et, count, 128), F32),
            dma((3,)),
            dma((group,)),
            dma((group,)),
            dma((n,)),
            dma((n,)),
            dma((2, n2, 2)),
            dma((n, 2)),
            dma((n, 2)),
            dma((n, 2)),
            dma((n_et,)),
            dma((n_et,)),
            dma((2, n2, 2)),
            dma((2, n2, 2)),
            dma((n,)),
            dma((n,)),
            dma((group,)),
            dma((group,)),
            dma((n_et,)),
            dma((n_et,)),
        ],
        compiler_params=pltpu.CompilerParams(
            collective_id=0, has_side_effects=True, vmem_limit_bytes=48 * 1024 * 1024
        ),
    )(expert_ids, gate_probs, tokens, out_grad, w_gate, w_up, w_down)


def solution(mesh):
    return jax.shard_map(
        body,
        mesh=mesh,
        in_specs=(
            P("de", "et"),
            P("de", None),
            P("de", None),
            P(None, ("de", "et")),
            P(None, ("de", "et")),
            P(("de", "et"), None),
            P("de", "et"),
        ),
        out_specs=(P("de", "et"), P("de", "et"), P("de", None)),
        check_vma=False,
    )
```

```python
import functools

import jax
import jax.numpy as jnp
from jax import lax
from jax.experimental import pallas as pl
from jax.experimental.pallas import tpu as pltpu
from jax.sharding import PartitionSpec as P

EXPERTS = 4
CAP = 5
SLOT = 8
Y_HI = 2
PARTS = 4
MESH = pl.DeviceIdType.MESH
F32 = jnp.float32
BF16 = jnp.bfloat16
HIGHEST = lax.Precision.HIGHEST


def dot(a, b, contract, precision=None):
    return lax.dot_general(
        a, b, ((contract[0], contract[1]), ((), ())), preferred_element_type=F32, precision=precision
    )


def fifth(p):
    return (p * 13) >> 6


def kernel(
    sizes,
    ids_hbm,
    probs_hbm,
    tok_hbm,
    grad_hbm,
    wg_hbm,
    wu_hbm,
    wd_hbm,
    mixed_ref,
    tgrad_ref,
    pgrad_ref,
    ids_ref,
    probs_ref,
    tok_ref,
    grad_ref,
    wgu,
    wdv,
    s1,
    r1,
    gb,
    acc_gu,
    acc_d,
    hid,
    dgu,
    tb,
    sr,
    rr,
    p2,
    s2,
    r2,
    pg,
    in_sem,
    w_sem,
    s1_s,
    s1_r,
    p1_s,
    p1_r,
    ag_s,
    ag_r,
    sh_s,
    sh_r,
    st_s,
    st_r,
    rs_s,
    rs_r,
    p2_s,
    p2_r,
    s2_s,
    s2_r,
    pg_s,
    pg_r,
):
    nx, yl, n = sizes
    n2 = n // 2
    pa = n // PARTS
    group = 2 * nx
    rows = group * CAP
    tokens, width = tok_ref.shape
    units = wdv.shape[0]
    de, et = lax.axis_index("de"), lax.axis_index("et")
    c = lax.rem(de, 2)
    y_lo = lax.rem(lax.div(de, 2), yl)
    x = lax.div(de, 2 * yl)
    y_hi, z = lax.div(et, n), lax.rem(et, n)
    y = y_hi * yl + y_lo
    me = x * 2 + c
    b0 = jnp.where(c == 0, y, z)
    a0 = jnp.where(c == 0, z, y)

    def wrap(v, m):
        return lax.rem(v + m, m)

    def device(x_, y_, z_, c_):
        return ((x_ * yl + lax.rem(y_, yl)) * 2 + c_, lax.div(y_, yl) * n + z_)

    def at_ba(b_, a_):
        return device(x, jnp.where(c == 0, b_, a_), jnp.where(c == 0, a_, b_), c)

    def at_group(idx):
        return device(lax.div(idx, 2), y, z, lax.rem(idx, 2))

    sibling = device(x, y, z, 1 - c)
    onward = (at_ba(wrap(b0 + 1, n), a0), at_ba(wrap(b0 - 1, n), a0))
    sends = []

    def remote(src, dst, s_sem, r_sem, to):
        return pltpu.make_async_remote_copy(
            src_ref=src, dst_ref=dst, send_sem=s_sem, recv_sem=r_sem, device_id=to, device_id_type=MESH
        )

    def send(src, dst, s_sem, r_sem, to):
        copy = remote(src, dst, s_sem, r_sem, to)
        copy.start()
        sends.append(copy)

    def arrived(dst, sem):
        pltpu.make_async_copy(dst, dst, sem).wait()

    barrier = pltpu.get_barrier_semaphore()
    peers = [at_group(wrap(me + i, group)) for i in range(1, group)]
    for i in range(1, n):
        peers.append(device(x, y, wrap(z + i, n), c))
        peers.append(device(x, wrap(y + i, n), z, c))
        peers.append(device(x, wrap(y + yl, n), wrap(z + i, n), c))
    inputs = [
        pltpu.make_async_copy(src, dst, in_sem.at[i])
        for i, (src, dst) in enumerate(
            ((ids_hbm, ids_ref), (probs_hbm, probs_ref), (tok_hbm, tok_ref), (grad_hbm, grad_ref))
        )
    ]
    for copy in inputs:
        copy.start()
    for peer in peers:
        pl.semaphore_signal(barrier, inc=1, device_id=peer, device_id_type=MESH)
    for copy in inputs:
        copy.wait()

    ids = [ids_ref[j : j + 1, :] for j in range(2)]
    probs = [probs_ref[j : j + 1, :] for j in range(2)]
    expert = lax.broadcasted_iota(jnp.int32, (8, tokens), 0)
    named = jnp.where((expert == ids[0]) | (expert == ids[1]), 1.0, 0.0)
    before = lax.broadcasted_iota(jnp.int32, (tokens, tokens), 0)
    after = lax.broadcasted_iota(jnp.int32, (tokens, tokens), 1)
    last = ((1,), (0,))
    rank = dot(named, jnp.where(before < after, 1.0, 0.0), last, HIGHEST)
    slots = lax.broadcasted_iota(jnp.int32, (nx * SLOT, tokens), 0).astype(F32)
    place = []
    for j in range(2):
        rank_j = jnp.sum(jnp.where(expert == ids[j], rank, 0.0), axis=0, keepdims=True)
        place.append(jnp.where(slots == ids[j].astype(F32) * SLOT + rank_j, 1.0, 0.0))
    both = place[0] + place[1]
    weight = jnp.sum(place[0] * probs[0] + place[1] * probs[1], axis=1, keepdims=True)
    xs = dot(both, tok_ref[...].astype(F32), last, HIGHEST)
    raw = dot(both, grad_ref[...].astype(F32), last, HIGHEST)
    gs = weight * raw
    for e in range(nx):
        block = slice(e * SLOT, (e + 1) * SLOT)
        s1[e] = jnp.concatenate([xs[block], gs[block]], axis=0).astype(BF16)

    pl.semaphore_wait(barrier, len(peers))

    for i in range(1, group):
        to = wrap(me + i, group)
        send(s1.at[lax.div(to, 2)], r1.at[me], s1_s.at[i], s1_r.at[i], at_group(to))
    loads = (
        pltpu.make_async_copy(wg_hbm, wgu.at[:, pl.ds(0, units)], w_sem.at[0]),
        pltpu.make_async_copy(wu_hbm, wgu.at[:, pl.ds(units, units)], w_sem.at[1]),
        pltpu.make_async_copy(wd_hbm, wdv, w_sem.at[2]),
    )
    for load in loads:
        load.start()
    r1[me] = s1[x]
    acc_gu[...] = jnp.zeros_like(acc_gu)
    acc_d[...] = jnp.zeros_like(acc_d)
    p = lax.broadcasted_iota(jnp.int32, (rows, group * 16), 0)
    col = lax.broadcasted_iota(jnp.int32, (rows, group * 16), 1)
    pick = jnp.where(col == p + 11 * fifth(p) + 8 * c, 1.0, 0.0).astype(BF16)
    for i in range(1, group):
        arrived(r1.at[wrap(me - i, group)], s1_r.at[i])
    staged = r1[...].reshape(group * 16, width)
    gb[c, b0, a0] = dot(pick, staged, last).astype(BF16)

    for i in range(1, n):
        send(gb.at[c, b0, a0], gb.at[c, b0, a0], p1_s.at[i], p1_r.at[a0], at_ba(b0, wrap(a0 + i, n)))

    def part(h):
        return pl.ds(h * pa, pa)

    def takes(h, d):
        return (h < PARTS // 2) == (d == 0)

    def unit(b_, h):
        return gb.at[c, b_, part(h)]

    def share(b_, h):
        send(unit(b_, h), unit(b_, h), sh_s.at[b_, h], sh_r.at[b_, h], sibling)

    o0 = jnp.where(c == 0, z, y)

    def around(v, s):
        return [wrap(v + s, n)] if s in (0, n2) else [wrap(v + s, n), wrap(v - s, n)]

    def multiply(s):
        for o_ in around(o0, s):
            for h in range(PARTS):
                arrived(gb.at[1 - c, o_, part(h)], sh_r.at[o_, h])
        for z_ in around(z, s):
            total = acc_d[...]
            for hi in range(Y_HI):
                g = jnp.concatenate([gb[1, z_, hi * yl + k] for k in range(yl)], axis=0)
                span = pl.ds(pl.multiple_of((hi * n + z_) * width, width), width)
                total = total + dot(g, wdv[:, span], ((1,), (1,)))
            acc_d[...] = total
        for y_ in around(y, s):
            hi, lo = lax.div(y_, yl), lax.rem(y_, yl)
            v = jnp.concatenate([gb[0, y_, k] for k in range(n)], axis=1)
            span = pl.ds(pl.multiple_of(hi * (n * width), n * width), n * width)
            acc_gu[lo] += dot(v, wgu[span, :], last)

    for h in range(PARTS):
        for a_ in range(h * pa, (h + 1) * pa):

            @pl.when(a0 != a_)
            def _():
                arrived(gb.at[c, b0, a_], p1_r.at[a_])

        for d in range(2):
            send(unit(b0, h), unit(b0, h), ag_s.at[d, 0, h], ag_r.at[b0, h], onward[d])
        share(b0, h)
    for load in loads:
        load.wait()
    for s in range(1, n2 + 1):
        for h in range(PARTS):
            for d in range(2):
                if s == n2 and not takes(h, d):
                    continue
                b_ = wrap(b0 - s, n) if d == 0 else wrap(b0 + s, n)
                arrived(unit(b_, h), ag_r.at[b_, h])
                if s < n2 - 1 or (s == n2 - 1 and takes(h, d)):
                    send(unit(b_, h), unit(b_, h), ag_s.at[d, s, h], ag_r.at[b_, h], onward[d])
                share(b_, h)
        multiply(s - 1)
    multiply(n2)

    both_rows = acc_gu[...].reshape(yl * rows, 2 * units)
    gate, up, d_hidden = both_rows[:, :units], both_rows[:, units:], acc_d[...]
    sig = jax.nn.sigmoid(gate)
    hidden = (gate * sig * up).astype(BF16)
    for k in range(yl):
        hid[k] = hidden[k * rows : (k + 1) * rows]
    dgu[:, :units] = (d_hidden * up * sig * (1.0 + gate * (1.0 - sig))).astype(BF16)
    dgu[:, units:] = (d_hidden * gate * sig).astype(BF16)

    def terms(s):
        for z_ in around(z, s):
            for hi in range(Y_HI):
                span = pl.ds(pl.multiple_of((hi * n + z_) * width, width), width)
                v = dot(dgu[...], wgu[span, :], ((1,), (1,))).astype(BF16)
                for k in range(yl):
                    tb[1, z_, hi * yl + k] = v[k * rows : (k + 1) * rows]
        for y_ in around(y, s):
            hi, lo = lax.div(y_, yl), lax.rem(y_, yl)
            span = pl.ds(pl.multiple_of(hi * (n * width), n * width), n * width)
            v = dot(hid[lo], wdv[:, span], last).astype(BF16)
            for k in range(n):
                tb[0, y_, k] = v[:, k * width : (k + 1) * width]
        for o_ in around(o0, s):
            send(tb.at[1 - c, o_], sr.at[o_], st_s.at[o_], st_r.at[o_], sibling)

    def own(t, h):
        return tb[c, t, part(h)].astype(F32) + sr[t, part(h)].astype(F32)

    terms(n2)
    terms(n2 - 1)
    for k in range(n2, 0, -1):
        for t in around(b0, k):
            arrived(sr.at[t], st_r.at[t])
        for h in range(PARTS):
            for d in range(2):
                if k == n2 and not takes(h, d):
                    continue
                t = wrap(b0 + k, n) if d == 0 else wrap(b0 - k, n)
                value = own(t, h)
                if k < n2 - 1 or (k == n2 - 1 and takes(h, d)):
                    arrived(rr.at[d, k, h], rs_r.at[d, k, h])
                    value = value + rr[d, k, h].astype(F32)
                tb[c, t, part(h)] = value.astype(BF16)
                send(
                    tb.at[c, t, part(h)],
                    rr.at[d, k - 1, h],
                    rs_s.at[d, k - 1, h],
                    rs_r.at[d, k - 1, h],
                    onward[d],
                )
        if k >= 2:
            terms(k - 2)
    arrived(sr.at[b0], st_r.at[b0])

    def along(a_):
        return remote(tb.at[c, b0, a_], p2.at[a0], p2_s.at[a_], p2_r.at[a0], at_ba(b0, a_))

    for h in range(PARTS):
        value = own(b0, h)
        for d in range(2):
            arrived(rr.at[d, 0, h], rs_r.at[d, 0, h])
            value = value + rr[d, 0, h].astype(F32)
        tb[c, b0, part(h)] = value.astype(BF16)
        for a_ in range(h * pa, (h + 1) * pa):

            @pl.when(a0 != a_)
            def _():
                along(a_).start()

    total = tb[c, b0, a0].astype(F32)
    for i in range(1, n):
        a_ = wrap(a0 - i, n)
        arrived(p2.at[a_], p2_r.at[a_])
        total = total + p2[a_].astype(F32)

    r = lax.broadcasted_iota(jnp.int32, (group * SLOT, rows), 0)
    p = lax.broadcasted_iota(jnp.int32, (group * SLOT, rows), 1)
    spread = jnp.where(r == p + 3 * fifth(p), 1.0, 0.0).astype(BF16)
    s2[...] = dot(spread, total.astype(BF16), last).reshape(group, SLOT, width).astype(BF16)
    for i in range(1, group):
        to = wrap(me + i, group)
        send(s2.at[to], r2.at[c, x], s2_s.at[i], s2_r.at[i], at_group(to))
    r2[c, x] = s2[me]
    for i in range(1, group):
        idx = wrap(me - i, group)
        arrived(r2.at[lax.rem(idx, 2), lax.div(idx, 2)], s2_r.at[i])

    first = ((0,), (0,))
    y_rows = r2[0].astype(F32).reshape(nx * SLOT, width)
    x_rows = r2[1].astype(F32).reshape(nx * SLOT, width)
    score = jnp.sum(raw * y_rows, axis=1, keepdims=True)
    for j in range(2):
        pg[et, j : j + 1, 0:tokens] = jnp.sum(place[j] * score, axis=0, keepdims=True)
    n_et = Y_HI * n
    for i in range(1, n_et):
        send(pg.at[et], pg.at[et], pg_s.at[i], pg_r.at[i], (de, wrap(et + i, n_et)))
    mixed_ref[...] = dot(both, weight * y_rows, first, HIGHEST).astype(BF16)
    tgrad_ref[...] = dot(both, x_rows, first, HIGHEST).astype(BF16)
    for i in range(1, n_et):
        arrived(pg.at[wrap(et - i, n_et)], pg_r.at[i])
    sums = pg[0, 0:2, 0:tokens]
    for i in range(1, n_et):
        sums = sums + pg[i, 0:2, 0:tokens]
    pgrad_ref[...] = sums
    for copy in sends:
        copy.wait_send()
    for a_ in range(n):

        @pl.when(a0 != a_)
        def _():
            along(a_).wait_send()


def body(tokens, expert_ids, gate_probs, w_gate, w_up, w_down, out_grad):
    n_de, n_et = lax.axis_size("de"), lax.axis_size("et")
    nx = EXPERTS
    yl = n_de // (2 * nx)
    n = n_et // Y_HI
    n2 = n // 2
    pa = n // PARTS
    group = 2 * nx
    rows = group * CAP
    count, width = tokens.shape
    depth, units = w_gate.shape
    slots = yl * rows
    vmem = pl.BlockSpec(memory_space=pltpu.VMEM)
    hbm = pl.BlockSpec(memory_space=pltpu.HBM)
    dma = pltpu.SemaphoreType.DMA
    mixed, token_grad, prob_grad = pl.pallas_call(
        functools.partial(kernel, (nx, yl, n)),
        out_shape=(
            jax.ShapeDtypeStruct((count, width), BF16),
            jax.ShapeDtypeStruct((count, width), BF16),
            jax.ShapeDtypeStruct((2, count), F32),
        ),
        in_specs=[hbm] * 7,
        out_specs=(vmem, vmem, vmem),
        scratch_shapes=[
            pltpu.VMEM((2, count), jnp.int32),
            pltpu.VMEM((2, count), F32),
            pltpu.VMEM((count, width), BF16),
            pltpu.VMEM((count, width), BF16),
            pltpu.VMEM((depth, 2 * units), BF16),
            pltpu.VMEM((units, depth), BF16),
            pltpu.VMEM((nx, 16, width), BF16),
            pltpu.VMEM((group, 16, width), BF16),
            pltpu.VMEM((2, n, n, rows, width), BF16),
            pltpu.VMEM((yl, rows, 2 * units), F32),
            pltpu.VMEM((slots, units), F32),
            pltpu.VMEM((yl, rows, units), BF16),
            pltpu.VMEM((slots, 2 * units), BF16),
            pltpu.VMEM((2, n, n, rows, width), BF16),
            pltpu.VMEM((n, n, rows, width), BF16),
            pltpu.VMEM((2, n2, PARTS, pa, rows, width), BF16),
            pltpu.VMEM((n, rows, width), BF16),
            pltpu.VMEM((group, SLOT, width), BF16),
            pltpu.VMEM((2, nx, SLOT, width), BF16),
            pltpu.VMEM((n_et, 8, 128), F32),
            dma((4,)),
            dma((3,)),
            dma((group,)),
            dma((group,)),
            dma((n,)),
            dma((n,)),
            dma((2, n2, PARTS)),
            dma((n, PARTS)),
            dma((n, PARTS)),
            dma((n, PARTS)),
            dma((n,)),
            dma((n,)),
            dma((2, n2, PARTS)),
            dma((2, n2, PARTS)),
            dma((n,)),
            dma((n,)),
            dma((group,)),
            dma((group,)),
            dma((n_et,)),
            dma((n_et,)),
        ],
        compiler_params=pltpu.CompilerParams(
            collective_id=0, has_side_effects=True, vmem_limit_bytes=56 * 1024 * 1024
        ),
    )(expert_ids.T, gate_probs.T, tokens, out_grad, w_gate, w_up, w_down)
    return mixed, token_grad, prob_grad.T


def solution(mesh):
    return jax.shard_map(
        body,
        mesh=mesh,
        in_specs=(
            P("de", "et"),
            P("de", None),
            P("de", None),
            P(None, ("de", "et")),
            P(None, ("de", "et")),
            P(("de", "et"), None),
            P("de", "et"),
        ),
        out_specs=(P("de", "et"), P("de", "et"), P("de", None)),
        check_vma=False,
    )
```

```python
import functools

import jax
import jax.numpy as jnp
from jax import lax
from jax.experimental import pallas as pl
from jax.experimental.pallas import tpu as pltpu
from jax.sharding import PartitionSpec as P

EXPERTS = 4
CAP = 5
SLOT = 8
Y_HI = 2
PARTS = 4
MESH = pl.DeviceIdType.MESH
F32 = jnp.float32
BF16 = jnp.bfloat16
HIGHEST = lax.Precision.HIGHEST


def dot(a, b, contract, precision=None):
    return lax.dot_general(
        a, b, ((contract[0], contract[1]), ((), ())), preferred_element_type=F32, precision=precision
    )


def fifth(p):
    return (p * 13) >> 6


def kernel(
    sizes,
    ids_hbm,
    probs_hbm,
    tok_hbm,
    grad_hbm,
    wg_hbm,
    wu_hbm,
    wd_hbm,
    mixed_ref,
    tgrad_ref,
    pgrad_ref,
    ids_ref,
    probs_ref,
    tok_ref,
    grad_ref,
    wgu,
    wdv,
    s1,
    r1,
    gb,
    acc_gu,
    acc_d,
    hid,
    dgu,
    tb,
    sr,
    rr,
    p2,
    s2,
    r2,
    sc_z,
    sc_y,
    sc_c,
    in_sem,
    w_sem,
    s1_s,
    s1_r,
    p1_s,
    p1_r,
    ag_s,
    ag_r,
    sh_s,
    sh_r,
    st_s,
    st_r,
    rs_s,
    rs_r,
    p2_s,
    p2_r,
    s2_s,
    s2_r,
    sc_s,
    sc_r,
):
    nx, yl, n = sizes
    n2 = n // 2
    pa = n // PARTS
    group = 2 * nx
    rows = group * CAP
    tokens, width = tok_ref.shape
    units = wdv.shape[0]
    de, et = lax.axis_index("de"), lax.axis_index("et")
    c = lax.rem(de, 2)
    y_lo = lax.rem(lax.div(de, 2), yl)
    x = lax.div(de, 2 * yl)
    y_hi, z = lax.div(et, n), lax.rem(et, n)
    y = y_hi * yl + y_lo
    me = x * 2 + c
    b0 = jnp.where(c == 0, y, z)
    a0 = jnp.where(c == 0, z, y)

    def wrap(v, m):
        return lax.rem(v + m, m)

    def device(x_, y_, z_, c_):
        return ((x_ * yl + lax.rem(y_, yl)) * 2 + c_, lax.div(y_, yl) * n + z_)

    def at_ba(b_, a_):
        return device(x, jnp.where(c == 0, b_, a_), jnp.where(c == 0, a_, b_), c)

    def at_group(idx):
        return device(lax.div(idx, 2), y, z, lax.rem(idx, 2))

    sibling = device(x, y, z, 1 - c)
    onward = (at_ba(wrap(b0 + 1, n), a0), at_ba(wrap(b0 - 1, n), a0))
    def remote(src, dst, s_sem, r_sem, to):
        return pltpu.make_async_remote_copy(
            src_ref=src, dst_ref=dst, send_sem=s_sem, recv_sem=r_sem, device_id=to, device_id_type=MESH
        )

    def send(src, dst, s_sem, r_sem, to):
        remote(src, dst, s_sem, r_sem, to).start()

    def arrived(dst, sem):
        pltpu.make_async_copy(dst, dst, sem).wait()

    barrier = pltpu.get_barrier_semaphore()
    peers = [at_group(wrap(me + i, group)) for i in range(1, group)]
    for i in range(1, n):
        peers.append(device(x, y, wrap(z + i, n), c))
        peers.append(device(x, wrap(y + i, n), z, c))
    inputs = [
        pltpu.make_async_copy(src, dst, in_sem.at[i])
        for i, (src, dst) in enumerate(
            ((ids_hbm, ids_ref), (probs_hbm, probs_ref), (tok_hbm, tok_ref), (grad_hbm, grad_ref))
        )
    ]
    for copy in inputs:
        copy.start()
    for peer in peers:
        pl.semaphore_signal(barrier, inc=1, device_id=peer, device_id_type=MESH)
    for copy in inputs:
        copy.wait()

    ids = [ids_ref[j : j + 1, :] for j in range(2)]
    probs = [probs_ref[j : j + 1, :] for j in range(2)]
    expert = lax.broadcasted_iota(jnp.int32, (8, tokens), 0)
    named = jnp.where((expert == ids[0]) | (expert == ids[1]), 1.0, 0.0)
    before = lax.broadcasted_iota(jnp.int32, (tokens, tokens), 0)
    after = lax.broadcasted_iota(jnp.int32, (tokens, tokens), 1)
    last = ((1,), (0,))
    strict = jnp.where(before < after, 1.0, 0.0).astype(BF16)
    rank = dot(named.astype(BF16), strict, last)
    slots = lax.broadcasted_iota(jnp.int32, (nx * SLOT, tokens), 0).astype(F32)
    place = []
    for j in range(2):
        rank_j = jnp.sum(jnp.where(expert == ids[j], rank, 0.0), axis=0, keepdims=True)
        place.append(jnp.where(slots == ids[j].astype(F32) * SLOT + rank_j, 1.0, 0.0))
    both = (place[0] + place[1]).astype(BF16)
    weight = jnp.sum(place[0] * probs[0] + place[1] * probs[1], axis=1, keepdims=True)
    xs = dot(both, tok_ref[...], last)
    gs = weight * dot(both, grad_ref[...], last)
    for e in range(nx):
        block = slice(e * SLOT, (e + 1) * SLOT)
        s1[e] = jnp.concatenate([xs[block], gs[block]], axis=0).astype(BF16)

    pl.semaphore_wait(barrier, len(peers))

    for i in range(1, group):
        to = wrap(me + i, group)
        send(s1.at[lax.div(to, 2)], r1.at[me], s1_s, s1_r, at_group(to))
    loads = (
        pltpu.make_async_copy(wg_hbm, wgu.at[:, pl.ds(0, units)], w_sem.at[0]),
        pltpu.make_async_copy(wu_hbm, wgu.at[:, pl.ds(units, units)], w_sem.at[1]),
        pltpu.make_async_copy(wd_hbm, wdv, w_sem.at[2]),
    )
    for load in loads:
        load.start()
    r1[me] = s1[x]
    acc_gu[...] = jnp.zeros_like(acc_gu)
    acc_d[...] = jnp.zeros_like(acc_d)
    p = lax.broadcasted_iota(jnp.int32, (rows, group * 16), 0)
    col = lax.broadcasted_iota(jnp.int32, (rows, group * 16), 1)
    pick = jnp.where(col == p + 11 * fifth(p) + 8 * c, 1.0, 0.0).astype(BF16)
    eye = jnp.where(before == after, 1.0, 0.0)
    turned = [dot(eye.astype(BF16), place[j].astype(BF16), ((1,), (1,))).astype(BF16) for j in range(2)]
    share_of = [jnp.sum(eye * probs[j], axis=1, keepdims=True) for j in range(2)]
    inverse = jnp.where(weight > 0.0, 1.0 / jnp.where(weight > 0.0, weight, 1.0), 0.0)
    arrived(r1.at[pl.ds(0, group - 1)], s1_r)
    staged = r1[...].reshape(group * 16, width)
    gb[c, b0, a0] = dot(pick, staged, last).astype(BF16)

    for i in range(1, n):
        send(gb.at[c, b0, a0], gb.at[c, b0, a0], p1_s, p1_r.at[a0], at_ba(b0, wrap(a0 + i, n)))

    def part(h):
        return pl.ds(h * pa, pa)

    def takes(h, d):
        return (h < PARTS // 2) == (d == 0)

    def unit(b_, h):
        return gb.at[c, b_, part(h)]

    def share(b_, h):
        send(unit(b_, h), unit(b_, h), sh_s, sh_r.at[b_], sibling)

    o0 = jnp.where(c == 0, z, y)

    def around(v, s):
        return [wrap(v + s, n)] if s in (0, n2) else [wrap(v + s, n), wrap(v - s, n)]

    def multiply(s):
        for o_ in around(o0, s):
            arrived(gb.at[1 - c, o_], sh_r.at[o_])
        for z_ in around(z, s):
            total = acc_d[...]
            for hi in range(Y_HI):
                g = jnp.concatenate([gb[1, z_, hi * yl + k] for k in range(yl)], axis=0)
                span = pl.ds(pl.multiple_of((hi * n + z_) * width, width), width)
                total = total + dot(g, wdv[:, span], ((1,), (1,)))
            acc_d[...] = total
        for y_ in around(y, s):
            hi, lo = lax.div(y_, yl), lax.rem(y_, yl)
            v = jnp.concatenate([gb[0, y_, k] for k in range(n)], axis=1)
            span = pl.ds(pl.multiple_of(hi * (n * width), n * width), n * width)
            acc_gu[lo] += dot(v, wgu[span, :], last)

    for h in range(PARTS):
        for a_ in range(h * pa, (h + 1) * pa):

            @pl.when(a0 != a_)
            def _():
                arrived(gb.at[c, b0, a_], p1_r.at[a_])

        for d in range(2):
            send(unit(b0, h), unit(b0, h), ag_s, ag_r.at[b0, h], onward[d])
        share(b0, h)
    for load in loads:
        load.wait()
    for s in range(1, n2 + 1):
        for h in range(PARTS):
            for d in range(2):
                if s == n2 and not takes(h, d):
                    continue
                b_ = wrap(b0 - s, n) if d == 0 else wrap(b0 + s, n)
                arrived(unit(b_, h), ag_r.at[b_, h])
                if s < n2 - 1 or (s == n2 - 1 and takes(h, d)):
                    send(unit(b_, h), unit(b_, h), ag_s, ag_r.at[b_, h], onward[d])
                share(b_, h)
        multiply(s - 1)
    multiply(n2)

    both_rows = acc_gu[...].reshape(yl * rows, 2 * units)
    gate, up, d_hidden = both_rows[:, :units], both_rows[:, units:], acc_d[...]
    sig = jax.nn.sigmoid(gate)
    hidden = (gate * sig * up).astype(BF16)
    for k in range(yl):
        hid[k] = hidden[k * rows : (k + 1) * rows]
    dgu[:, :units] = (d_hidden * up * sig * (1.0 + gate * (1.0 - sig))).astype(BF16)
    dgu[:, units:] = (d_hidden * gate * sig).astype(BF16)
    ones = jnp.ones((8, units), F32)
    sc_z[z, :, 0 : yl * rows] = dot(ones, hidden.astype(F32) * d_hidden, ((1,), (1,)), HIGHEST)

    def score_step(stage):
        if stage == 0:
            for i in range(1, n):
                send(sc_z.at[z], sc_z.at[z], sc_s.at[0], sc_r.at[0], device(x, y, wrap(z + i, n), c))
        if stage == 1:
            arrived(sc_z.at[pl.ds(0, n - 1)], sc_r.at[0])
            sc_y[y] = jnp.sum(sc_z[...], axis=0)
            for i in range(1, n):
                send(sc_y.at[y], sc_y.at[y], sc_s.at[1], sc_r.at[1], device(x, wrap(y + i, n), z, c))
        if stage == 2:
            arrived(sc_y.at[pl.ds(0, n - 1)], sc_r.at[1])
            sc_c[c] = jnp.sum(sc_y[...], axis=0)
            send(sc_c.at[c], sc_c.at[c], sc_s.at[2], sc_r.at[2], sibling)

    def terms(s):
        for z_ in around(z, s):
            for hi in range(Y_HI):
                span = pl.ds(pl.multiple_of((hi * n + z_) * width, width), width)
                v = dot(dgu[...], wgu[span, :], ((1,), (1,))).astype(BF16)
                for k in range(yl):
                    tb[1, z_, hi * yl + k] = v[k * rows : (k + 1) * rows]
        for y_ in around(y, s):
            hi, lo = lax.div(y_, yl), lax.rem(y_, yl)
            span = pl.ds(pl.multiple_of(hi * (n * width), n * width), n * width)
            v = dot(hid[lo], wdv[:, span], last).astype(BF16)
            for k in range(n):
                tb[0, y_, k] = v[:, k * width : (k + 1) * width]
        for o_ in around(o0, s):
            send(tb.at[1 - c, o_], sr.at[o_], st_s, st_r.at[o_], sibling)

    def own(t, h):
        return tb[c, t, part(h)].astype(F32) + sr[t, part(h)].astype(F32)

    terms(n2)
    terms(n2 - 1)
    score_step(0)
    for k in range(n2, 0, -1):
        for t in around(b0, k):
            arrived(sr.at[t], st_r.at[t])
        for h in range(PARTS):
            for d in range(2):
                if k == n2 and not takes(h, d):
                    continue
                t = wrap(b0 + k, n) if d == 0 else wrap(b0 - k, n)
                value = own(t, h)
                if k < n2 - 1 or (k == n2 - 1 and takes(h, d)):
                    arrived(rr.at[d, k, h], rs_r.at[d, k, h])
                    value = value + rr[d, k, h].astype(F32)
                tb[c, t, part(h)] = value.astype(BF16)
                send(
                    tb.at[c, t, part(h)],
                    rr.at[d, k - 1, h],
                    rs_s,
                    rs_r.at[d, k - 1, h],
                    onward[d],
                )
        if k >= 2:
            terms(k - 2)
        score_step(n2 + 1 - k)
    arrived(sr.at[b0], st_r.at[b0])

    def along(a_):
        return remote(tb.at[c, b0, a_], p2.at[a0], p2_s, p2_r, at_ba(b0, a_))

    for h in range(PARTS):
        value = own(b0, h)
        for d in range(2):
            arrived(rr.at[d, 0, h], rs_r.at[d, 0, h])
            value = value + rr[d, 0, h].astype(F32)
        tb[c, b0, part(h)] = value.astype(BF16)
        for a_ in range(h * pa, (h + 1) * pa):

            @pl.when(a0 != a_)
            def _():
                along(a_).start()

    arrived(sc_c.at[0], sc_r.at[2])
    scores = sc_c[0, 0:1, :] + sc_c[1, 0:1, :]
    lane = lax.broadcasted_iota(jnp.int32, (rows, scores.shape[1]), 1)
    row = lax.broadcasted_iota(jnp.int32, (rows, scores.shape[1]), 0)
    score = jnp.sum(jnp.where(lane == row + y_lo * rows, scores, 0.0), axis=1, keepdims=True)
    high = score.astype(BF16).astype(F32)
    lane = lane[:, :128]
    ending = jnp.where(lane == 0, high, jnp.where(lane == 1, score - high, 0.0)).astype(BF16)
    arrived(p2.at[pl.ds(0, n - 1)], p2_r)
    total = tb[c, b0, a0].astype(F32)
    for i in range(1, n):
        total = total + p2[wrap(a0 - i, n)].astype(F32)

    r = lax.broadcasted_iota(jnp.int32, (group * SLOT, rows), 0)
    p = lax.broadcasted_iota(jnp.int32, (group * SLOT, rows), 1)
    spread = jnp.where(r == p + 3 * fifth(p), 1.0, 0.0).astype(BF16)
    full = jnp.concatenate([total.astype(BF16), ending], axis=1)
    s2[...] = dot(spread, full, last).reshape(group, SLOT, width + 128).astype(BF16)
    for i in range(1, group):
        to = wrap(me + i, group)
        send(s2.at[to], r2.at[c, x], s2_s, s2_r, at_group(to))
    r2[c, x] = s2[me]
    arrived(s2.at[pl.ds(0, group - 1)], s2_r)

    y_rows = r2[0].astype(F32).reshape(nx * SLOT, width + 128)
    x_rows = r2[1].astype(F32).reshape(nx * SLOT, width + 128)
    score = (y_rows[:, width : width + 1] + y_rows[:, width + 1 : width + 2]) * inverse
    for j in range(2):
        pgrad_ref[j : j + 1, :] = jnp.sum(place[j] * score, axis=0, keepdims=True)
    y_rows = y_rows[:, :width].astype(BF16)
    x_rows = x_rows[:, :width].astype(BF16)
    mixed_ref[...] = (
        share_of[0] * dot(turned[0], y_rows, last) + share_of[1] * dot(turned[1], y_rows, last)
    ).astype(BF16)
    tgrad_ref[...] = dot(turned[0] + turned[1], x_rows, last).astype(BF16)
    for done, sem in (
        (r1.at[pl.ds(0, group - 1)], s1_s),
        (gb.at[0, 0, pl.ds(0, n - 1)], p1_s),
        (gb.at[0, pl.ds(0, n - 1)], ag_s),
        (gb.at[0], sh_s),
        (gb.at[0], st_s),
        (gb.at[0, pl.ds(0, n - 1)], rs_s),
        (gb.at[0, 0, pl.ds(0, n - 1)], p2_s),
        (s2.at[pl.ds(0, group - 1)], s2_s),
        (sc_z.at[pl.ds(0, n - 1)], sc_s.at[0]),
        (sc_y.at[pl.ds(0, n - 1)], sc_s.at[1]),
        (sc_c.at[0], sc_s.at[2]),
    ):
        arrived(done, sem)


def body(tokens, expert_ids, gate_probs, w_gate, w_up, w_down, out_grad):
    n_de, n_et = lax.axis_size("de"), lax.axis_size("et")
    nx = EXPERTS
    yl = n_de // (2 * nx)
    n = n_et // Y_HI
    n2 = n // 2
    pa = n // PARTS
    group = 2 * nx
    rows = group * CAP
    count, width = tokens.shape
    depth, units = w_gate.shape
    slots = yl * rows
    lanes = pl.cdiv(slots, 128) * 128
    vmem = pl.BlockSpec(memory_space=pltpu.VMEM)
    hbm = pl.BlockSpec(memory_space=pltpu.HBM)
    dma = pltpu.SemaphoreType.DMA
    mixed, token_grad, prob_grad = pl.pallas_call(
        functools.partial(kernel, (nx, yl, n)),
        out_shape=(
            jax.ShapeDtypeStruct((count, width), BF16),
            jax.ShapeDtypeStruct((count, width), BF16),
            jax.ShapeDtypeStruct((2, count), F32),
        ),
        in_specs=[hbm] * 7,
        out_specs=(vmem, vmem, vmem),
        scratch_shapes=[
            pltpu.VMEM((2, count), jnp.int32),
            pltpu.VMEM((2, count), F32),
            pltpu.VMEM((count, width), BF16),
            pltpu.VMEM((count, width), BF16),
            pltpu.VMEM((depth, 2 * units), BF16),
            pltpu.VMEM((units, depth), BF16),
            pltpu.VMEM((nx, 16, width), BF16),
            pltpu.VMEM((group, 16, width), BF16),
            pltpu.VMEM((2, n, n, rows, width), BF16),
            pltpu.VMEM((yl, rows, 2 * units), F32),
            pltpu.VMEM((slots, units), F32),
            pltpu.VMEM((yl, rows, units), BF16),
            pltpu.VMEM((slots, 2 * units), BF16),
            pltpu.VMEM((2, n, n, rows, width), BF16),
            pltpu.VMEM((n, n, rows, width), BF16),
            pltpu.VMEM((2, n2, PARTS, pa, rows, width), BF16),
            pltpu.VMEM((n, rows, width), BF16),
            pltpu.VMEM((group, SLOT, width + 128), BF16),
            pltpu.VMEM((2, nx, SLOT, width + 128), BF16),
            pltpu.VMEM((n, 8, lanes), F32),
            pltpu.VMEM((n, 8, lanes), F32),
            pltpu.VMEM((2, 8, lanes), F32),
            dma((4,)),
            dma((3,)),
            dma(()),
            dma(()),
            dma(()),
            dma((n,)),
            dma(()),
            dma((n, PARTS)),
            dma(()),
            dma((n,)),
            dma(()),
            dma((n,)),
            dma(()),
            dma((2, n2, PARTS)),
            dma(()),
            dma(()),
            dma(()),
            dma(()),
            dma((3,)),
            dma((3,)),
        ],
        compiler_params=pltpu.CompilerParams(
            collective_id=0, has_side_effects=True, vmem_limit_bytes=56 * 1024 * 1024
        ),
    )(expert_ids.T, gate_probs.T, tokens, out_grad, w_gate, w_up, w_down)
    return mixed, token_grad, prob_grad.T


def solution(mesh):
    return jax.shard_map(
        body,
        mesh=mesh,
        in_specs=(
            P("de", "et"),
            P("de", None),
            P("de", None),
            P(None, ("de", "et")),
            P(None, ("de", "et")),
            P(("de", "et"), None),
            P("de", "et"),
        ),
        out_specs=(P("de", "et"), P("de", "et"), P("de", None)),
        check_vma=False,
    )
```

```python
import functools

import jax
import jax.numpy as jnp
from jax import lax
from jax.experimental import pallas as pl
from jax.experimental.pallas import tpu as pltpu
from jax.sharding import PartitionSpec as P

EXPERTS = 4
CAP = 5
SLOT = 8
Y_HI = 2
PARTS = 8
MESH = pl.DeviceIdType.MESH
F32 = jnp.float32
BF16 = jnp.bfloat16
HIGHEST = lax.Precision.HIGHEST


def dot(a, b, contract, precision=None):
    return lax.dot_general(
        a, b, ((contract[0], contract[1]), ((), ())), preferred_element_type=F32, precision=precision
    )


def fifth(p):
    return (p * 13) >> 6


def kernel(
    sizes,
    ids_hbm,
    probs_hbm,
    tok_hbm,
    grad_hbm,
    wg_hbm,
    wu_hbm,
    wd_hbm,
    mixed_ref,
    tgrad_ref,
    pgrad_ref,
    ids_ref,
    probs_ref,
    tok_ref,
    grad_ref,
    wgu,
    wdv,
    s1,
    r1,
    gb,
    acc_gu,
    acc_d,
    hid,
    dgu,
    tb,
    sr,
    rr,
    p2,
    s2,
    r2,
    sc_z,
    sc_y,
    sc_c,
    in_sem,
    w_sem,
    s1_s,
    s1_r,
    p1_s,
    p1_r,
    ag_s,
    ag_r,
    sh_s,
    sh_r,
    st_s,
    st_r,
    rs_s,
    rs_r,
    p2_s,
    p2_r,
    s2_s,
    s2_r,
    sc_s,
    sc_r,
):
    nx, yl, n = sizes
    n2 = n // 2
    pa = n // PARTS
    group = 2 * nx
    rows = group * CAP
    tokens, width = tok_ref.shape
    units = wdv.shape[0]
    de, et = lax.axis_index("de"), lax.axis_index("et")
    c = lax.rem(de, 2)
    y_lo = lax.rem(lax.div(de, 2), yl)
    x = lax.div(de, 2 * yl)
    y_hi, z = lax.div(et, n), lax.rem(et, n)
    y = y_hi * yl + y_lo
    me = x * 2 + c
    b0 = jnp.where(c == 0, y, z)
    a0 = jnp.where(c == 0, z, y)

    def wrap(v, m):
        return lax.rem(v + m, m)

    def device(x_, y_, z_, c_):
        return ((x_ * yl + lax.rem(y_, yl)) * 2 + c_, lax.div(y_, yl) * n + z_)

    def at_ba(b_, a_):
        return device(x, jnp.where(c == 0, b_, a_), jnp.where(c == 0, a_, b_), c)

    def at_group(idx):
        return device(lax.div(idx, 2), y, z, lax.rem(idx, 2))

    sibling = device(x, y, z, 1 - c)
    onward = (at_ba(wrap(b0 + 1, n), a0), at_ba(wrap(b0 - 1, n), a0))
    def remote(src, dst, s_sem, r_sem, to):
        return pltpu.make_async_remote_copy(
            src_ref=src, dst_ref=dst, send_sem=s_sem, recv_sem=r_sem, device_id=to, device_id_type=MESH
        )

    def send(src, dst, s_sem, r_sem, to):
        remote(src, dst, s_sem, r_sem, to).start()

    def arrived(dst, sem):
        pltpu.make_async_copy(dst, dst, sem).wait()

    barrier = pltpu.get_barrier_semaphore()
    peers = [at_group(wrap(me + i, group)) for i in range(1, group)]
    for i in range(1, n):
        peers.append(device(x, y, wrap(z + i, n), c))
        peers.append(device(x, wrap(y + i, n), z, c))
    inputs = [
        pltpu.make_async_copy(src, dst, in_sem.at[i])
        for i, (src, dst) in enumerate(
            ((ids_hbm, ids_ref), (probs_hbm, probs_ref), (tok_hbm, tok_ref), (grad_hbm, grad_ref))
        )
    ]
    for copy in inputs:
        copy.start()
    for peer in peers:
        pl.semaphore_signal(barrier, inc=1, device_id=peer, device_id_type=MESH)
    for copy in inputs:
        copy.wait()

    ids = [ids_ref[j : j + 1, :] for j in range(2)]
    probs = [probs_ref[j : j + 1, :] for j in range(2)]
    expert = lax.broadcasted_iota(jnp.int32, (8, tokens), 0)
    named = jnp.where((expert == ids[0]) | (expert == ids[1]), 1.0, 0.0)
    before = lax.broadcasted_iota(jnp.int32, (tokens, tokens), 0)
    after = lax.broadcasted_iota(jnp.int32, (tokens, tokens), 1)
    last = ((1,), (0,))
    strict = jnp.where(before < after, 1.0, 0.0).astype(BF16)
    rank = dot(named.astype(BF16), strict, last)
    slots = lax.broadcasted_iota(jnp.int32, (nx * SLOT, tokens), 0).astype(F32)
    place = []
    for j in range(2):
        rank_j = jnp.sum(jnp.where(expert == ids[j], rank, 0.0), axis=0, keepdims=True)
        place.append(jnp.where(slots == ids[j].astype(F32) * SLOT + rank_j, 1.0, 0.0))
    both = (place[0] + place[1]).astype(BF16)
    weight = jnp.sum(place[0] * probs[0] + place[1] * probs[1], axis=1, keepdims=True)
    xs = dot(both, tok_ref[...], last)
    gs = weight * dot(both, grad_ref[...], last)
    for e in range(nx):
        block = slice(e * SLOT, (e + 1) * SLOT)
        s1[e] = jnp.concatenate([xs[block], gs[block]], axis=0).astype(BF16)

    pl.semaphore_wait(barrier, len(peers))

    for i in range(1, group):
        to = wrap(me + i, group)
        send(s1.at[lax.div(to, 2)], r1.at[me], s1_s, s1_r, at_group(to))
    loads = (
        pltpu.make_async_copy(wg_hbm, wgu.at[:, pl.ds(0, units)], w_sem.at[0]),
        pltpu.make_async_copy(wu_hbm, wgu.at[:, pl.ds(units, units)], w_sem.at[1]),
        pltpu.make_async_copy(wd_hbm, wdv, w_sem.at[2]),
    )
    for load in loads:
        load.start()
    r1[me] = s1[x]
    acc_gu[...] = jnp.zeros_like(acc_gu)
    acc_d[...] = jnp.zeros_like(acc_d)
    p = lax.broadcasted_iota(jnp.int32, (rows, group * 16), 0)
    col = lax.broadcasted_iota(jnp.int32, (rows, group * 16), 1)
    pick = jnp.where(col == p + 11 * fifth(p) + 8 * c, 1.0, 0.0).astype(BF16)
    arrived(r1.at[pl.ds(0, group - 1)], s1_r)
    staged = r1[...].reshape(group * 16, width)
    gb[c, b0, a0] = dot(pick, staged, last).astype(BF16)

    for i in range(1, n):
        send(gb.at[c, b0, a0], gb.at[c, b0, a0], p1_s, p1_r.at[a0], at_ba(b0, wrap(a0 + i, n)))

    def part(h):
        return pl.ds(h * pa, pa)

    def takes(h, d):
        return (h < PARTS // 2) == (d == 0)

    def unit(b_, h):
        return gb.at[c, b_, part(h)]

    def share(b_, h):
        send(unit(b_, h), unit(b_, h), sh_s, sh_r.at[b_], sibling)

    o0 = jnp.where(c == 0, z, y)

    def around(v, s):
        return [wrap(v + s, n)] if s in (0, n2) else [wrap(v + s, n), wrap(v - s, n)]

    def multiply(s):
        for o_ in around(o0, s):
            arrived(gb.at[1 - c, o_], sh_r.at[o_])
        for z_ in around(z, s):
            total = acc_d[...]
            for hi in range(Y_HI):
                g = jnp.concatenate([gb[1, z_, hi * yl + k] for k in range(yl)], axis=0)
                span = pl.ds(pl.multiple_of((hi * n + z_) * width, width), width)
                total = total + dot(g, wdv[:, span], ((1,), (1,)))
            acc_d[...] = total
        for y_ in around(y, s):
            hi, lo = lax.div(y_, yl), lax.rem(y_, yl)
            v = jnp.concatenate([gb[0, y_, k] for k in range(n)], axis=1)
            span = pl.ds(pl.multiple_of(hi * (n * width), n * width), n * width)
            acc_gu[lo] += dot(v, wgu[span, :], last)

    for h in range(PARTS):
        for a_ in range(h * pa, (h + 1) * pa):

            @pl.when(a0 != a_)
            def _():
                arrived(gb.at[c, b0, a_], p1_r.at[a_])

        for d in range(2):
            send(unit(b0, h), unit(b0, h), ag_s, ag_r.at[b0, h], onward[d])
        share(b0, h)
    for load in loads:
        load.wait()
    for s in range(1, n2 + 1):
        for h in range(PARTS):
            for d in range(2):
                if s == n2 and not takes(h, d):
                    continue
                b_ = wrap(b0 - s, n) if d == 0 else wrap(b0 + s, n)
                arrived(unit(b_, h), ag_r.at[b_, h])
                if s < n2 - 1 or (s == n2 - 1 and takes(h, d)):
                    send(unit(b_, h), unit(b_, h), ag_s, ag_r.at[b_, h], onward[d])
                share(b_, h)
        multiply(s - 1)
    multiply(n2)

    both_rows = acc_gu[...].reshape(yl * rows, 2 * units)
    gate, up, d_hidden = both_rows[:, :units], both_rows[:, units:], acc_d[...]
    sig = jax.nn.sigmoid(gate)
    hidden = (gate * sig * up).astype(BF16)
    for k in range(yl):
        hid[k] = hidden[k * rows : (k + 1) * rows]
    dgu[:, :units] = (d_hidden * up * sig * (1.0 + gate * (1.0 - sig))).astype(BF16)
    dgu[:, units:] = (d_hidden * gate * sig).astype(BF16)

    def score_step(stage):
        if stage == 0:
            ones = jnp.ones((8, units), F32)
            sc_z[z, :, 0 : yl * rows] = dot(ones, hidden.astype(F32) * d_hidden, ((1,), (1,)), HIGHEST)
            for i in range(1, n):
                send(sc_z.at[z], sc_z.at[z], sc_s.at[0], sc_r.at[0], device(x, y, wrap(z + i, n), c))
        if stage == 1:
            arrived(sc_z.at[pl.ds(0, n - 1)], sc_r.at[0])
            sc_y[y] = jnp.sum(sc_z[...], axis=0)
            for i in range(1, n):
                send(sc_y.at[y], sc_y.at[y], sc_s.at[1], sc_r.at[1], device(x, wrap(y + i, n), z, c))
        if stage == 2:
            arrived(sc_y.at[pl.ds(0, n - 1)], sc_r.at[1])
            sc_c[c] = jnp.sum(sc_y[...], axis=0)
            send(sc_c.at[c], sc_c.at[c], sc_s.at[2], sc_r.at[2], sibling)

    def terms(s):
        for z_ in around(z, s):
            for hi in range(Y_HI):
                span = pl.ds(pl.multiple_of((hi * n + z_) * width, width), width)
                v = dot(dgu[...], wgu[span, :], ((1,), (1,))).astype(BF16)
                for k in range(yl):
                    tb[1, z_, hi * yl + k] = v[k * rows : (k + 1) * rows]
        for y_ in around(y, s):
            hi, lo = lax.div(y_, yl), lax.rem(y_, yl)
            span = pl.ds(pl.multiple_of(hi * (n * width), n * width), n * width)
            v = dot(hid[lo], wdv[:, span], last).astype(BF16)
            for k in range(n):
                tb[0, y_, k] = v[:, k * width : (k + 1) * width]
        for o_ in around(o0, s):
            send(tb.at[1 - c, o_], sr.at[o_], st_s, st_r.at[o_], sibling)

    def own(t, h):
        return tb[c, t, part(h)].astype(F32) + sr[t, part(h)].astype(F32)

    terms(n2)
    terms(n2 - 1)
    score_step(0)
    for k in range(n2, 0, -1):
        for t in around(b0, k):
            arrived(sr.at[t], st_r.at[t])
        for h in range(PARTS):
            for d in range(2):
                if k == n2 and not takes(h, d):
                    continue
                t = wrap(b0 + k, n) if d == 0 else wrap(b0 - k, n)
                value = own(t, h)
                if k < n2 - 1 or (k == n2 - 1 and takes(h, d)):
                    arrived(rr.at[d, k, h], rs_r.at[d, k, h])
                    value = value + rr[d, k, h].astype(F32)
                tb[c, t, part(h)] = value.astype(BF16)
                send(
                    tb.at[c, t, part(h)],
                    rr.at[d, k - 1, h],
                    rs_s,
                    rs_r.at[d, k - 1, h],
                    onward[d],
                )
        if k >= 2:
            terms(k - 2)
        score_step(n2 + 1 - k)
    arrived(sr.at[b0], st_r.at[b0])

    def along(a_):
        return remote(tb.at[c, b0, a_], p2.at[a0], p2_s, p2_r, at_ba(b0, a_))

    for h in range(PARTS):
        value = own(b0, h)
        for d in range(2):
            arrived(rr.at[d, 0, h], rs_r.at[d, 0, h])
            value = value + rr[d, 0, h].astype(F32)
        tb[c, b0, part(h)] = value.astype(BF16)
        for a_ in range(h * pa, (h + 1) * pa):

            @pl.when(a0 != a_)
            def _():
                along(a_).start()

    arrived(sc_c.at[0], sc_r.at[2])
    scores = sc_c[0, 0:1, :] + sc_c[1, 0:1, :]
    lane = lax.broadcasted_iota(jnp.int32, (rows, scores.shape[1]), 1)
    row = lax.broadcasted_iota(jnp.int32, (rows, scores.shape[1]), 0)
    score = jnp.sum(jnp.where(lane == row + y_lo * rows, scores, 0.0), axis=1, keepdims=True)
    high = score.astype(BF16).astype(F32)
    lane = lane[:, :128]
    ending = jnp.where(lane == 0, high, jnp.where(lane == 1, score - high, 0.0)).astype(BF16)
    arrived(p2.at[pl.ds(0, n - 1)], p2_r)
    total = tb[c, b0, a0].astype(F32)
    for i in range(1, n):
        total = total + p2[wrap(a0 - i, n)].astype(F32)

    r = lax.broadcasted_iota(jnp.int32, (group * SLOT, rows), 0)
    p = lax.broadcasted_iota(jnp.int32, (group * SLOT, rows), 1)
    spread = jnp.where(r == p + 3 * fifth(p), 1.0, 0.0).astype(BF16)
    full = jnp.concatenate([total.astype(BF16), ending], axis=1)
    s2[...] = dot(spread, full, last).reshape(group, SLOT, width + 128).astype(BF16)
    for i in range(1, group):
        to = wrap(me + i, group)
        send(s2.at[to], r2.at[c, x], s2_s, s2_r, at_group(to))
    r2[c, x] = s2[me]
    eye = jnp.where(before == after, 1.0, 0.0)
    turned = [dot(eye.astype(BF16), place[j].astype(BF16), ((1,), (1,))).astype(BF16) for j in range(2)]
    share_of = [jnp.sum(eye * probs[j], axis=1, keepdims=True) for j in range(2)]
    inverse = jnp.where(weight > 0.0, 1.0 / jnp.where(weight > 0.0, weight, 1.0), 0.0)
    arrived(s2.at[pl.ds(0, group - 1)], s2_r)

    y_rows = r2[0].astype(F32).reshape(nx * SLOT, width + 128)
    x_rows = r2[1].astype(F32).reshape(nx * SLOT, width + 128)
    score = (y_rows[:, width : width + 1] + y_rows[:, width + 1 : width + 2]) * inverse
    for j in range(2):
        pgrad_ref[j : j + 1, :] = jnp.sum(place[j] * score, axis=0, keepdims=True)
    y_rows = y_rows[:, :width].astype(BF16)
    x_rows = x_rows[:, :width].astype(BF16)
    mixed_ref[...] = (
        share_of[0] * dot(turned[0], y_rows, last) + share_of[1] * dot(turned[1], y_rows, last)
    ).astype(BF16)
    tgrad_ref[...] = dot(turned[0] + turned[1], x_rows, last).astype(BF16)
    for done, sem in (
        (r1.at[pl.ds(0, group - 1)], s1_s),
        (gb.at[0, 0, pl.ds(0, n - 1)], p1_s),
        (gb.at[0, pl.ds(0, n - 1)], ag_s),
        (gb.at[0], sh_s),
        (gb.at[0], st_s),
        (gb.at[0, pl.ds(0, n - 1)], rs_s),
        (gb.at[0, 0, pl.ds(0, n - 1)], p2_s),
        (s2.at[pl.ds(0, group - 1)], s2_s),
        (sc_z.at[pl.ds(0, n - 1)], sc_s.at[0]),
        (sc_y.at[pl.ds(0, n - 1)], sc_s.at[1]),
        (sc_c.at[0], sc_s.at[2]),
    ):
        arrived(done, sem)


def settle(mixed_in, tgrad_in, pgrad_in, mixed_ref, tgrad_ref, pgrad_ref, sem):
    copies = [
        pltpu.make_async_copy(src, dst, sem.at[i])
        for i, (src, dst) in enumerate(((mixed_in, mixed_ref), (tgrad_in, tgrad_ref), (pgrad_in, pgrad_ref)))
    ]
    for copy in copies:
        copy.start()
    for copy in copies:
        copy.wait()


def body(tokens, expert_ids, gate_probs, w_gate, w_up, w_down, out_grad):
    n_de, n_et = lax.axis_size("de"), lax.axis_size("et")
    nx = EXPERTS
    yl = n_de // (2 * nx)
    n = n_et // Y_HI
    n2 = n // 2
    pa = n // PARTS
    group = 2 * nx
    rows = group * CAP
    count, width = tokens.shape
    depth, units = w_gate.shape
    slots = yl * rows
    lanes = pl.cdiv(slots, 128) * 128
    vmem = pl.BlockSpec(memory_space=pltpu.VMEM)
    hbm = pl.BlockSpec(memory_space=pltpu.HBM)
    dma = pltpu.SemaphoreType.DMA
    mixed, token_grad, prob_grad = pl.pallas_call(
        functools.partial(kernel, (nx, yl, n)),
        out_shape=(
            jax.ShapeDtypeStruct((count, width), BF16),
            jax.ShapeDtypeStruct((count, width), BF16),
            jax.ShapeDtypeStruct((2, count), F32),
        ),
        in_specs=[hbm] * 7,
        out_specs=(vmem, vmem, vmem),
        scratch_shapes=[
            pltpu.VMEM((2, count), jnp.int32),
            pltpu.VMEM((2, count), F32),
            pltpu.VMEM((count, width), BF16),
            pltpu.VMEM((count, width), BF16),
            pltpu.VMEM((depth, 2 * units), BF16),
            pltpu.VMEM((units, depth), BF16),
            pltpu.VMEM((nx, 16, width), BF16),
            pltpu.VMEM((group, 16, width), BF16),
            pltpu.VMEM((2, n, n, rows, width), BF16),
            pltpu.VMEM((yl, rows, 2 * units), F32),
            pltpu.VMEM((slots, units), F32),
            pltpu.VMEM((yl, rows, units), BF16),
            pltpu.VMEM((slots, 2 * units), BF16),
            pltpu.VMEM((2, n, n, rows, width), BF16),
            pltpu.VMEM((n, n, rows, width), BF16),
            pltpu.VMEM((2, n2, PARTS, pa, rows, width), BF16),
            pltpu.VMEM((n, rows, width), BF16),
            pltpu.VMEM((group, SLOT, width + 128), BF16),
            pltpu.VMEM((2, nx, SLOT, width + 128), BF16),
            pltpu.VMEM((n, 8, lanes), F32),
            pltpu.VMEM((n, 8, lanes), F32),
            pltpu.VMEM((2, 8, lanes), F32),
            dma((4,)),
            dma((3,)),
            dma(()),
            dma(()),
            dma(()),
            dma((n,)),
            dma(()),
            dma((n, PARTS)),
            dma(()),
            dma((n,)),
            dma(()),
            dma((n,)),
            dma(()),
            dma((2, n2, PARTS)),
            dma(()),
            dma(()),
            dma(()),
            dma(()),
            dma((3,)),
            dma((3,)),
        ],
        compiler_params=pltpu.CompilerParams(
            collective_id=0, has_side_effects=True, vmem_limit_bytes=56 * 1024 * 1024
        ),
    )(expert_ids.T, gate_probs.T, tokens, out_grad, w_gate, w_up, w_down)
    mixed, token_grad, prob_grad = pl.pallas_call(
        settle,
        out_shape=tuple(jax.ShapeDtypeStruct(v.shape, v.dtype) for v in (mixed, token_grad, prob_grad)),
        in_specs=[hbm] * 3,
        out_specs=(hbm, hbm, hbm),
        scratch_shapes=[dma((3,))],
        compiler_params=pltpu.CompilerParams(vmem_limit_bytes=56 * 1024 * 1024),
    )(mixed, token_grad, prob_grad)
    return mixed, token_grad, prob_grad.T


def solution(mesh):
    return jax.shard_map(
        body,
        mesh=mesh,
        in_specs=(
            P("de", "et"),
            P("de", None),
            P("de", None),
            P(None, ("de", "et")),
            P(None, ("de", "et")),
            P(("de", "et"), None),
            P("de", "et"),
        ),
        out_specs=(P("de", "et"), P("de", "et"), P("de", None)),
        check_vma=False,
    )
```

```python
import functools

import jax
import jax.numpy as jnp
from jax import lax
from jax.experimental import pallas as pl
from jax.experimental.pallas import tpu as pltpu
from jax.sharding import PartitionSpec as P

EXPERTS = 4
CAP = 5
SLOT = 8
Y_HI = 2
MESH = pl.DeviceIdType.MESH
F32 = jnp.float32
BF16 = jnp.bfloat16
HIGHEST = lax.Precision.HIGHEST


def dot(a, b, contract, precision=None):
    return lax.dot_general(
        a, b, ((contract[0], contract[1]), ((), ())), preferred_element_type=F32, precision=precision
    )


def fifth(p):
    return (p * 13) >> 6


def kernel(
    sizes,
    ids_hbm,
    probs_hbm,
    tok_hbm,
    grad_hbm,
    wg_hbm,
    wu_hbm,
    wd_hbm,
    mixed_ref,
    tgrad_ref,
    pgrad_ref,
    ids_ref,
    probs_ref,
    tok_ref,
    grad_ref,
    wgu,
    wdv,
    s1,
    r1,
    gb,
    acc_gu,
    acc_d,
    hid,
    dgu,
    tb,
    sr,
    rr,
    p2,
    s2,
    r2,
    sc_z,
    sc_y,
    sc_c,
    in_sem,
    w_sem,
    s1_s,
    s1_r,
    p1_s,
    p1_r,
    ag_s,
    ag_r,
    sh_s,
    sh_r,
    st_s,
    st_r,
    rs_s,
    rs_r,
    p2_s,
    p2_r,
    s2_s,
    s2_r,
    sc_s,
    sc_r,
):
    nx, yl, n = sizes
    n2 = n // 2
    pa = 1
    group = 2 * nx
    rows = group * CAP
    tokens, width = tok_ref.shape
    units = wdv.shape[0]
    de, et = lax.axis_index("de"), lax.axis_index("et")
    c = lax.rem(de, 2)
    y_lo = lax.rem(lax.div(de, 2), yl)
    x = lax.div(de, 2 * yl)
    y_hi, z = lax.div(et, n), lax.rem(et, n)
    y = y_hi * yl + y_lo
    me = x * 2 + c
    b0 = jnp.where(c == 0, y, z)
    a0 = jnp.where(c == 0, z, y)

    def wrap(v, m):
        return lax.rem(v + m, m)

    def device(x_, y_, z_, c_):
        return ((x_ * yl + lax.rem(y_, yl)) * 2 + c_, lax.div(y_, yl) * n + z_)

    def at_ba(b_, a_):
        return device(x, jnp.where(c == 0, b_, a_), jnp.where(c == 0, a_, b_), c)

    def at_group(idx):
        return device(lax.div(idx, 2), y, z, lax.rem(idx, 2))

    sibling = device(x, y, z, 1 - c)
    onward = (at_ba(wrap(b0 + 1, n), a0), at_ba(wrap(b0 - 1, n), a0))
    def remote(src, dst, s_sem, r_sem, to):
        return pltpu.make_async_remote_copy(
            src_ref=src, dst_ref=dst, send_sem=s_sem, recv_sem=r_sem, device_id=to, device_id_type=MESH
        )

    def send(src, dst, s_sem, r_sem, to):
        remote(src, dst, s_sem, r_sem, to).start()

    def arrived(dst, sem):
        pltpu.make_async_copy(dst, dst, sem).wait()

    barrier = pltpu.get_barrier_semaphore()
    peers = [at_group(wrap(me + i, group)) for i in range(1, group)]
    for i in range(1, n):
        peers.append(device(x, y, wrap(z + i, n), c))
        peers.append(device(x, wrap(y + i, n), z, c))
    inputs = [
        pltpu.make_async_copy(src, dst, in_sem.at[i])
        for i, (src, dst) in enumerate(
            ((ids_hbm, ids_ref), (probs_hbm, probs_ref), (tok_hbm, tok_ref), (grad_hbm, grad_ref))
        )
    ]
    for copy in inputs:
        copy.start()
    for peer in peers:
        pl.semaphore_signal(barrier, inc=1, device_id=peer, device_id_type=MESH)
    for copy in inputs:
        copy.wait()

    ids = [ids_ref[j : j + 1, :] for j in range(2)]
    probs = [probs_ref[j : j + 1, :] for j in range(2)]
    expert = lax.broadcasted_iota(jnp.int32, (8, tokens), 0)
    named = jnp.where((expert == ids[0]) | (expert == ids[1]), 1.0, 0.0)
    before = lax.broadcasted_iota(jnp.int32, (tokens, tokens), 0)
    after = lax.broadcasted_iota(jnp.int32, (tokens, tokens), 1)
    last = ((1,), (0,))
    strict = jnp.where(before < after, 1.0, 0.0).astype(BF16)
    rank = dot(named.astype(BF16), strict, last)
    slots = lax.broadcasted_iota(jnp.int32, (nx * SLOT, tokens), 0).astype(F32)
    place = []
    for j in range(2):
        rank_j = jnp.sum(jnp.where(expert == ids[j], rank, 0.0), axis=0, keepdims=True)
        place.append(jnp.where(slots == ids[j].astype(F32) * SLOT + rank_j, 1.0, 0.0))
    both = (place[0] + place[1]).astype(BF16)
    weight = jnp.sum(place[0] * probs[0] + place[1] * probs[1], axis=1, keepdims=True)
    xs = dot(both, tok_ref[...], last)
    gs = weight * dot(both, grad_ref[...], last)
    for e in range(nx):
        block = slice(e * SLOT, (e + 1) * SLOT)
        s1[e] = jnp.concatenate([xs[block], gs[block]], axis=0).astype(BF16)

    pl.semaphore_wait(barrier, len(peers))

    for i in range(1, group):
        to = wrap(me + i, group)
        send(s1.at[lax.div(to, 2)], r1.at[me], s1_s, s1_r, at_group(to))
    loads = (
        pltpu.make_async_copy(wg_hbm, wgu.at[:, pl.ds(0, units)], w_sem.at[0]),
        pltpu.make_async_copy(wu_hbm, wgu.at[:, pl.ds(units, units)], w_sem.at[1]),
        pltpu.make_async_copy(wd_hbm, wdv, w_sem.at[2]),
    )
    for load in loads:
        load.start()
    r1[me] = s1[x]
    acc_gu[...] = jnp.zeros_like(acc_gu)
    acc_d[...] = jnp.zeros_like(acc_d)
    p = lax.broadcasted_iota(jnp.int32, (rows, group * 16), 0)
    col = lax.broadcasted_iota(jnp.int32, (rows, group * 16), 1)
    pick = jnp.where(col == p + 11 * fifth(p) + 8 * c, 1.0, 0.0).astype(BF16)
    arrived(r1.at[pl.ds(0, group - 1)], s1_r)
    staged = r1[...].reshape(group * 16, width)
    gb[c, b0, a0] = dot(pick, staged, last).astype(BF16)

    for i in range(1, n):
        send(gb.at[c, b0, a0], gb.at[c, b0, a0], p1_s, p1_r.at[a0], at_ba(b0, wrap(a0 + i, n)))

    offsets = [0] + [v for i in range(1, n2) for v in (i, -i)] + [n2]
    pieces = [wrap(a0 + v, n) if v else a0 for v in offsets]

    def part(h):
        return pl.ds(h * pa, pa)

    def takes(h, d):
        return (h < n // 2) == (d == 0)

    def unit(b_, h):
        return gb.at[c, b_, pieces[h]]

    def share(b_, h):
        send(unit(b_, h), unit(b_, h), sh_s, sh_r.at[b_], sibling)

    o0 = jnp.where(c == 0, z, y)

    def around(v, s):
        return [wrap(v + s, n)] if s in (0, n2) else [wrap(v + s, n), wrap(v - s, n)]

    def multiply(s):
        for o_ in around(o0, s):
            arrived(gb.at[1 - c, o_], sh_r.at[o_])
        for z_ in around(z, s):
            total = acc_d[...]
            for hi in range(Y_HI):
                g = jnp.concatenate([gb[1, z_, hi * yl + k] for k in range(yl)], axis=0)
                span = pl.ds(pl.multiple_of((hi * n + z_) * width, width), width)
                total = total + dot(g, wdv[:, span], ((1,), (1,)))
            acc_d[...] = total
        for y_ in around(y, s):
            hi, lo = lax.div(y_, yl), lax.rem(y_, yl)
            v = jnp.concatenate([gb[0, y_, k] for k in range(n)], axis=1)
            span = pl.ds(pl.multiple_of(hi * (n * width), n * width), n * width)
            acc_gu[lo] += dot(v, wgu[span, :], last)

    for h in range(n):
        if h:
            arrived(unit(b0, h), p1_r.at[pieces[h]])
        for d in range(2):
            send(unit(b0, h), unit(b0, h), ag_s, ag_r.at[b0, h], onward[d])
        share(b0, h)
    for load in loads:
        load.wait()
    for s in range(1, n2 + 1):
        for h in range(n):
            for d in range(2):
                if s == n2 and not takes(h, d):
                    continue
                b_ = wrap(b0 - s, n) if d == 0 else wrap(b0 + s, n)
                arrived(unit(b_, h), ag_r.at[b_, h])
                if s < n2 - 1 or (s == n2 - 1 and takes(h, d)):
                    send(unit(b_, h), unit(b_, h), ag_s, ag_r.at[b_, h], onward[d])
                share(b_, h)
        multiply(s - 1)
    multiply(n2)

    both_rows = acc_gu[...].reshape(yl * rows, 2 * units)
    gate, up, d_hidden = both_rows[:, :units], both_rows[:, units:], acc_d[...]
    sig = jax.nn.sigmoid(gate)
    hidden = (gate * sig * up).astype(BF16)
    for k in range(yl):
        hid[k] = hidden[k * rows : (k + 1) * rows]
    dgu[:, :units] = (d_hidden * up * sig * (1.0 + gate * (1.0 - sig))).astype(BF16)
    dgu[:, units:] = (d_hidden * gate * sig).astype(BF16)

    def score_step(stage):
        if stage == 0:
            ones = jnp.ones((8, units), F32)
            sc_z[z, :, 0 : yl * rows] = dot(ones, hidden.astype(F32) * d_hidden, ((1,), (1,)), HIGHEST)
            for i in range(1, n):
                send(sc_z.at[z], sc_z.at[z], sc_s.at[0], sc_r.at[0], device(x, y, wrap(z + i, n), c))
        if stage == 1:
            arrived(sc_z.at[pl.ds(0, n - 1)], sc_r.at[0])
            sc_y[y] = jnp.sum(sc_z[...], axis=0)
            for i in range(1, n):
                send(sc_y.at[y], sc_y.at[y], sc_s.at[1], sc_r.at[1], device(x, wrap(y + i, n), z, c))
        if stage == 2:
            arrived(sc_y.at[pl.ds(0, n - 1)], sc_r.at[1])
            sc_c[c] = jnp.sum(sc_y[...], axis=0)
            send(sc_c.at[c], sc_c.at[c], sc_s.at[2], sc_r.at[2], sibling)

    def terms(s):
        for z_ in around(z, s):
            for hi in range(Y_HI):
                span = pl.ds(pl.multiple_of((hi * n + z_) * width, width), width)
                v = dot(dgu[...], wgu[span, :], ((1,), (1,))).astype(BF16)
                for k in range(yl):
                    tb[1, z_, hi * yl + k] = v[k * rows : (k + 1) * rows]
        for y_ in around(y, s):
            hi, lo = lax.div(y_, yl), lax.rem(y_, yl)
            span = pl.ds(pl.multiple_of(hi * (n * width), n * width), n * width)
            v = dot(hid[lo], wdv[:, span], last).astype(BF16)
            for k in range(n):
                tb[0, y_, k] = v[:, k * width : (k + 1) * width]
        for o_ in around(o0, s):
            send(tb.at[1 - c, o_], sr.at[o_], st_s, st_r.at[o_], sibling)

    def own(t, h):
        return tb[c, t, part(h)].astype(F32) + sr[t, part(h)].astype(F32)

    terms(n2)
    terms(n2 - 1)
    score_step(0)
    for k in range(n2, 0, -1):
        for t in around(b0, k):
            arrived(sr.at[t], st_r.at[t])
        for h in range(n):
            for d in range(2):
                if k == n2 and not takes(h, d):
                    continue
                t = wrap(b0 + k, n) if d == 0 else wrap(b0 - k, n)
                value = own(t, h)
                if k < n2 - 1 or (k == n2 - 1 and takes(h, d)):
                    arrived(rr.at[d, k, h], rs_r.at[d, k, h])
                    value = value + rr[d, k, h].astype(F32)
                tb[c, t, part(h)] = value.astype(BF16)
                send(
                    tb.at[c, t, part(h)],
                    rr.at[d, k - 1, h],
                    rs_s,
                    rs_r.at[d, k - 1, h],
                    onward[d],
                )
        if k >= 2:
            terms(k - 2)
        score_step(n2 + 1 - k)
    arrived(sr.at[b0], st_r.at[b0])

    def along(a_):
        return remote(tb.at[c, b0, a_], p2.at[a0], p2_s, p2_r, at_ba(b0, a_))

    for h in range(n):
        value = own(b0, h)
        for d in range(2):
            arrived(rr.at[d, 0, h], rs_r.at[d, 0, h])
            value = value + rr[d, 0, h].astype(F32)
        tb[c, b0, part(h)] = value.astype(BF16)
        for a_ in range(h * pa, (h + 1) * pa):

            @pl.when(a0 != a_)
            def _():
                along(a_).start()

    arrived(sc_c.at[0], sc_r.at[2])
    scores = sc_c[0, 0:1, :] + sc_c[1, 0:1, :]
    lane = lax.broadcasted_iota(jnp.int32, (rows, scores.shape[1]), 1)
    row = lax.broadcasted_iota(jnp.int32, (rows, scores.shape[1]), 0)
    score = jnp.sum(jnp.where(lane == row + y_lo * rows, scores, 0.0), axis=1, keepdims=True)
    high = score.astype(BF16).astype(F32)
    lane = lane[:, :128]
    ending = jnp.where(lane == 0, high, jnp.where(lane == 1, score - high, 0.0)).astype(BF16)
    arrived(p2.at[pl.ds(0, n - 1)], p2_r)
    total = tb[c, b0, a0].astype(F32)
    for i in range(1, n):
        total = total + p2[wrap(a0 - i, n)].astype(F32)

    r = lax.broadcasted_iota(jnp.int32, (group * SLOT, rows), 0)
    p = lax.broadcasted_iota(jnp.int32, (group * SLOT, rows), 1)
    spread = jnp.where(r == p + 3 * fifth(p), 1.0, 0.0).astype(BF16)
    full = jnp.concatenate([total.astype(BF16), ending], axis=1)
    s2[...] = dot(spread, full, last).reshape(group, SLOT, width + 128).astype(BF16)
    for i in range(1, group):
        to = wrap(me + i, group)
        send(s2.at[to], r2.at[c, x], s2_s, s2_r, at_group(to))
    r2[c, x] = s2[me]
    eye = jnp.where(before == after, 1.0, 0.0)
    turned = [dot(eye.astype(BF16), place[j].astype(BF16), ((1,), (1,))).astype(BF16) for j in range(2)]
    share_of = [jnp.sum(eye * probs[j], axis=1, keepdims=True) for j in range(2)]
    inverse = jnp.where(weight > 0.0, 1.0 / jnp.where(weight > 0.0, weight, 1.0), 0.0)
    arrived(s2.at[pl.ds(0, group - 1)], s2_r)

    y_rows = r2[0].astype(F32).reshape(nx * SLOT, width + 128)
    x_rows = r2[1].astype(F32).reshape(nx * SLOT, width + 128)
    score = (y_rows[:, width : width + 1] + y_rows[:, width + 1 : width + 2]) * inverse
    for j in range(2):
        pgrad_ref[j : j + 1, :] = jnp.sum(place[j] * score, axis=0, keepdims=True)
    y_rows = y_rows[:, :width].astype(BF16)
    x_rows = x_rows[:, :width].astype(BF16)
    mixed_ref[...] = (
        share_of[0] * dot(turned[0], y_rows, last) + share_of[1] * dot(turned[1], y_rows, last)
    ).astype(BF16)
    tgrad_ref[...] = dot(turned[0] + turned[1], x_rows, last).astype(BF16)
    for done, sem in (
        (r1.at[pl.ds(0, group - 1)], s1_s),
        (gb.at[0, 0, pl.ds(0, n - 1)], p1_s),
        (gb.at[0, pl.ds(0, n - 1)], ag_s),
        (gb.at[0], sh_s),
        (gb.at[0], st_s),
        (gb.at[0, pl.ds(0, n - 1)], rs_s),
        (gb.at[0, 0, pl.ds(0, n - 1)], p2_s),
        (s2.at[pl.ds(0, group - 1)], s2_s),
        (sc_z.at[pl.ds(0, n - 1)], sc_s.at[0]),
        (sc_y.at[pl.ds(0, n - 1)], sc_s.at[1]),
        (sc_c.at[0], sc_s.at[2]),
    ):
        arrived(done, sem)


def settle(mixed_in, tgrad_in, pgrad_in, mixed_ref, tgrad_ref, pgrad_ref, sem):
    copies = [
        pltpu.make_async_copy(src, dst, sem.at[i])
        for i, (src, dst) in enumerate(((mixed_in, mixed_ref), (tgrad_in, tgrad_ref), (pgrad_in, pgrad_ref)))
    ]
    for copy in copies:
        copy.start()
    for copy in copies:
        copy.wait()


def body(tokens, expert_ids, gate_probs, w_gate, w_up, w_down, out_grad):
    n_de, n_et = lax.axis_size("de"), lax.axis_size("et")
    nx = EXPERTS
    yl = n_de // (2 * nx)
    n = n_et // Y_HI
    n2 = n // 2
    pa = 1
    group = 2 * nx
    rows = group * CAP
    count, width = tokens.shape
    depth, units = w_gate.shape
    slots = yl * rows
    lanes = pl.cdiv(slots, 128) * 128
    vmem = pl.BlockSpec(memory_space=pltpu.VMEM)
    hbm = pl.BlockSpec(memory_space=pltpu.HBM)
    dma = pltpu.SemaphoreType.DMA
    mixed, token_grad, prob_grad = pl.pallas_call(
        functools.partial(kernel, (nx, yl, n)),
        out_shape=(
            jax.ShapeDtypeStruct((count, width), BF16),
            jax.ShapeDtypeStruct((count, width), BF16),
            jax.ShapeDtypeStruct((2, count), F32),
        ),
        in_specs=[hbm] * 7,
        out_specs=(vmem, vmem, vmem),
        scratch_shapes=[
            pltpu.VMEM((2, count), jnp.int32),
            pltpu.VMEM((2, count), F32),
            pltpu.VMEM((count, width), BF16),
            pltpu.VMEM((count, width), BF16),
            pltpu.VMEM((depth, 2 * units), BF16),
            pltpu.VMEM((units, depth), BF16),
            pltpu.VMEM((nx, 16, width), BF16),
            pltpu.VMEM((group, 16, width), BF16),
            pltpu.VMEM((2, n, n, rows, width), BF16),
            pltpu.VMEM((yl, rows, 2 * units), F32),
            pltpu.VMEM((slots, units), F32),
            pltpu.VMEM((yl, rows, units), BF16),
            pltpu.VMEM((slots, 2 * units), BF16),
            pltpu.VMEM((2, n, n, rows, width), BF16),
            pltpu.VMEM((n, n, rows, width), BF16),
            pltpu.VMEM((2, n2, n, pa, rows, width), BF16),
            pltpu.VMEM((n, rows, width), BF16),
            pltpu.VMEM((group, SLOT, width + 128), BF16),
            pltpu.VMEM((2, nx, SLOT, width + 128), BF16),
            pltpu.VMEM((n, 8, lanes), F32),
            pltpu.VMEM((n, 8, lanes), F32),
            pltpu.VMEM((2, 8, lanes), F32),
            dma((4,)),
            dma((3,)),
            dma(()),
            dma(()),
            dma(()),
            dma((n,)),
            dma(()),
            dma((n, n)),
            dma(()),
            dma((n,)),
            dma(()),
            dma((n,)),
            dma(()),
            dma((2, n2, n)),
            dma(()),
            dma(()),
            dma(()),
            dma(()),
            dma((3,)),
            dma((3,)),
        ],
        compiler_params=pltpu.CompilerParams(
            collective_id=0, has_side_effects=True, vmem_limit_bytes=56 * 1024 * 1024
        ),
    )(expert_ids.T, gate_probs.T, tokens, out_grad, w_gate, w_up, w_down)
    mixed, token_grad, prob_grad = pl.pallas_call(
        settle,
        out_shape=tuple(jax.ShapeDtypeStruct(v.shape, v.dtype) for v in (mixed, token_grad, prob_grad)),
        in_specs=[hbm] * 3,
        out_specs=(hbm, hbm, hbm),
        scratch_shapes=[dma((3,))],
        compiler_params=pltpu.CompilerParams(vmem_limit_bytes=56 * 1024 * 1024),
    )(mixed, token_grad, prob_grad)
    return mixed, token_grad, prob_grad.T


def solution(mesh):
    return jax.shard_map(
        body,
        mesh=mesh,
        in_specs=(
            P("de", "et"),
            P("de", None),
            P("de", None),
            P(None, ("de", "et")),
            P(None, ("de", "et")),
            P(("de", "et"), None),
            P("de", "et"),
        ),
        out_specs=(P("de", "et"), P("de", "et"), P("de", None)),
        check_vma=False,
    )
```
